256 devices in a mesh: patch: 64 (over z, x, core), band: 4 (over y).
Axes of the slice: x: 4, y: 4, z: 8, core: 2. Of those that a mesh axis runs over, the one named last changes fastest.
Arguments:
- exposures: bfloat16 [2048, 4, 128, 128], P('patch', 'band'), may hold values from -6 to 6
- psf_taps: bfloat16 [2048, 4, 2, 7], P('patch', 'band'), may hold values from -0.15 to 1, as said below
- warp_rows: bfloat16 [2048, 4, 128, 128], P('patch', 'band'), may hold values from -0.2 to 1, as said below
- warp_cols: bfloat16 [2048, 4, 128, 128], P('patch', 'band'), may hold values from -0.2 to 1, as said below
- routes: int32 [4, 2048, 1], P('band'), may hold values from 0 to 63; in each aligned block of 32 rows (0 to 31, 32 to 63, ..., all dimensions but the last counted through in order) at most 2 rows name the same one
- offsets: int32 [4, 2048, 2], P('band'), may hold values from 0 to 384
- weights: float32 [4, 2048], P('band'), may hold values from 0.1 to 2
- det_weight: bfloat16 [64, 100], replicated, may hold values from -0.625 to 0.625
- det_bias: float32 [64], replicated, may hold values from -3 to 3
Outputs:
- coadd: bfloat16 [64, 4, 512, 512], P('patch', 'band')
- detection: bfloat16 [64, 64, 512, 512], P('patch', None, 'band')
The draws below stay inside these ranges and needn't reach their ends.
Inputs may be any that keep to these rules, and one draw needn't show every extreme that they name: `routes`: in each aligned block of 32 tiles of a band (the tiles of one device) no patch is named more than 2 times; over all bands together every patch is named by some tile. `psf_taps`: the centre tap (index 3) lies between 0.6 and 1.0, the others between -0.15 and 0.15. `warp_rows`: Lanczos-3 resampling matrices. `warp_cols`: Lanczos-3 resampling matrices.
All inputs are finite; a program needn't handle non-finite values.
Results may differ from the reference program's by a relative error of at most 0.007.
Values may be sent and summed in bfloat16 or wider, within the bound.
No kernel may reach another device: no remote copies, remote signals or barrier semaphores. Data moves between devices by JAX's collectives and lax.ppermute only.
A program may use at most 128 MiB of HBM per device.

```python
import math
import jax
import jax.numpy as jnp
import numpy as np
from jax import lax

S = 128
TAPS = 7
CH = 64
PS = 512
E_DEV = 32
PATCHES = 64
BANDS = 4
TILES = 2048
CAP = 2


def lanczos_draw(key, low_start):
    first, second = jax.random.split(key)
    start = jax.random.uniform(first, (TILES, BANDS, 1, 1), jnp.float32, low_start, 1.0)
    stretch = jax.random.uniform(second, (TILES, BANDS, 1, 1), jnp.float32, 0.0, 0.02)
    across = jnp.arange(S, dtype=jnp.float32)
    source = start + across[:, None] * (1.0 - stretch)
    distance = source - across[None, :]
    value = jnp.where(jnp.abs(distance) < 3.0, jnp.sinc(distance) * jnp.sinc(distance / 3.0), 0.0)
    return value.astype(jnp.bfloat16)


def draw_warp_rows(key, part):
    low_start = 0.0
    return lanczos_draw(jax.random.fold_in(key, 11), low_start)


def draw_warp_cols(key, part):
    low_start = 0.0
    return lanczos_draw(jax.random.fold_in(key, 23), low_start)


def draw_psf_taps(key, part):
    first, second = jax.random.split(jax.random.fold_in(key, 5))
    shape = (TILES, BANDS, 2, TAPS)
    centre_low = 0.6
    spread = jax.random.uniform(first, shape, jnp.float32, -0.145, 0.145)
    centre = jax.random.uniform(second, shape, jnp.float32, centre_low, 1.0)
    position = jnp.arange(TAPS)
    return jnp.where(position == TAPS // 2, centre, spread).astype(jnp.bfloat16)


def plant(entries, own_key, smallest, largest):
    longest = entries.shape.index(max(entries.shape))
    spots = []
    for shift in (0, 1):
        where = [jax.random.randint(jax.random.fold_in(own_key, axis), (), 0, length) for axis, length in enumerate(entries.shape)]
        where[longest] = (where[longest] + shift) % entries.shape[longest]
        spots.append(tuple(where))
    return entries.at[spots[0]].set(smallest).at[spots[1]].set(largest)


def block_scale(stream_key, dims, cuts, low, high):
    gain, own = 1.0, jax.random.fold_in(stream_key, 6)
    for dim, blocks in cuts:
        heights = jnp.exp(jax.random.uniform(jax.random.fold_in(own, dim), (blocks,), jnp.float32, low / len(cuts), high / len(cuts)))
        gain = gain * jnp.repeat(heights, dims[dim] // blocks).reshape([-1 if axis == dim else 1 for axis in range(len(dims))])
    return gain


def routed_block(own_key, own, number, rows, count, top, most, skew):
    sequence = jax.random.permutation(own_key, count)
    packed, usual = load_shares(count, rows * top, most, skew, True), load_shares(count, rows * top, most, skew, False)
    places = jnp.arange(count)

    def named(sizes, rotation):
        used = int((sizes > 0).sum())
        fixed = max(1, used // 4)
        moved = fixed + (places - fixed + rotation * (used - fixed)) % max(1, count - fixed)
        return jnp.zeros((count,), jnp.int32).at[sequence[jnp.where(places < fixed, places, moved)]].set(jnp.asarray(sizes, jnp.int32))

    sizes = jnp.where(number % 4 == 0, named(packed, number // 4), named(usual, number - number // 4 - 1))
    mixed = jax.random.permutation(jax.random.fold_in(own, 3), count)
    donor, taker = mixed[0:count // 2 * 2:2], mixed[1:count // 2 * 2:2]
    room = jnp.minimum(sizes[donor] - 1, most - sizes[taker]) // 2
    room = jnp.where((donor == sequence[0]) | (taker == sequence[0]) | (sizes[taker] == 0), 0, jnp.maximum(room, 0))
    moved = jax.random.randint(jax.random.fold_in(own, 4), (count // 2,), 0, 1 << 20) % (room + 1)
    sizes = sizes.at[donor].add(-moved).at[taker].add(moved)
    items = jnp.searchsorted(jnp.cumsum(sizes), jnp.arange(rows * top), side="right").astype(jnp.int32)
    grid = items.reshape(top, rows).T
    grid = grid[jax.random.permutation(jax.random.fold_in(own, 1), rows)]
    rotation = jax.random.randint(jax.random.fold_in(own, 2), (rows, 1), 0, top)
    return jnp.take_along_axis(grid, (jnp.arange(top)[None, :] + rotation) % top, axis=1)


def load_shares(amount, total, bound, skew, full):
    portions = [(1 << 20) // math.isqrt(standing ** skew) + 1 for standing in range(1, amount + 1)]
    largest = bound if full else min(bound, max(-(-total // amount), total * portions[0] // sum(portions)))
    least = 1 if total - largest >= amount - 1 else 0
    given, surplus = [largest] + [least] * (amount - 1), total - largest - least * (amount - 1)
    while surplus > 0:
        movable = [i for i in range(1, amount) if given[i] < largest] or [i for i in range(1, amount) if given[i] < bound]
        mass, remaining = sum([portions[i] for i in movable]), surplus
        for i in movable:
            more = min(bound - given[i], max(1, remaining * portions[i] // mass), surplus)
            given[i] = given[i] + more
            surplus = surplus - more
    return np.array(given)


def gaussian(key, extent, deviation, bound, shards=(), kind=jnp.bfloat16):
    factor_of = block_scale(key, extent, shards, -0.22, 0.18) if shards else 1.0
    drawn = jax.random.normal(key, extent, jnp.float32) * deviation * factor_of
    return jnp.minimum(jnp.maximum(drawn, -bound), bound).astype(kind)


def setup_inputs(seed: int = 0) -> dict:
    arg_keys = jax.random.split(jax.random.key(seed), 10)
    exposures = gaussian(arg_keys[0], (TILES, BANDS, S, S), 1.0, 6.0, ((0, 64), (1, 4)))
    psf_taps = draw_psf_taps(jax.random.fold_in(arg_keys[9], 71), 0)
    warp_rows = draw_warp_rows(jax.random.fold_in(arg_keys[9], 71), 0)
    warp_cols = draw_warp_cols(jax.random.fold_in(arg_keys[9], 71), 0)
    routes_keys = jax.random.split(jax.random.fold_in(arg_keys[4], 1), BANDS * TILES // E_DEV)
    routes_turns = jax.random.permutation(jax.random.fold_in(arg_keys[4], 3), BANDS * TILES // E_DEV)
    routes = jax.vmap(lambda own, number: routed_block(jax.random.fold_in(arg_keys[4], 2), own, number, E_DEV, PATCHES, 1, CAP, 1))(routes_keys, routes_turns).reshape((BANDS, TILES, 1))
    offsets = plant(jax.random.randint(arg_keys[5], (BANDS, TILES, 2), 0, PS - S + 1), jax.random.fold_in(arg_keys[5], 1), 0, PS - S).astype(jnp.int32)
    weights = jnp.clip(jnp.exp(math.log(2.0) - 2.9957323 * jax.random.uniform(arg_keys[6], (BANDS, TILES), jnp.float32) ** block_scale(arg_keys[6], (BANDS, TILES), ((0, 4),), -0.2, 0.2)), 0.1, 2.0)
    det_weight = gaussian(arg_keys[7], (CH, BANDS * 25), (BANDS * 25) ** -0.5, 0.625)
    det_bias = gaussian(arg_keys[8], (CH,), 0.5, 3.0, (), jnp.float32)
    return dict(exposures=exposures, psf_taps=psf_taps, warp_rows=warp_rows, warp_cols=warp_cols, routes=routes, offsets=offsets, weights=weights, det_weight=det_weight, det_bias=det_bias)


def band_matrix(taps, tile_side):
    across = jnp.arange(tile_side)
    offset_diag = across[None, :] - across[:, None] + taps.shape[-1] // 2
    result = jnp.zeros((taps.shape[0], tile_side, tile_side), taps.dtype)
    for tap_index in range(taps.shape[-1]):
        result = result + jnp.where((offset_diag == tap_index)[None], taps[:, tap_index, None, None], jnp.zeros((), taps.dtype))
    return result


def warp_band(tile_data, taps, rows_warp, cols_warp, tile_weight):
    psf_rows = band_matrix(taps[:, 0].astype(jnp.float32), S)
    psf_cols = band_matrix(taps[:, 1].astype(jnp.float32), S)
    half_done = jnp.einsum("eij,ekj->eik", tile_data.astype(jnp.float32), psf_cols).astype(jnp.bfloat16)
    matched = jnp.einsum("eij,ejk->eik", psf_rows, half_done.astype(jnp.float32)).astype(jnp.bfloat16)
    across_cols = jnp.einsum("eij,ekj->eik", matched.astype(jnp.float32), cols_warp.astype(jnp.float32)).astype(jnp.bfloat16)
    product = jnp.einsum("eij,ejk->eik", rows_warp.astype(jnp.float32), across_cols.astype(jnp.float32))
    return (tile_weight[:, None, None] * product).astype(jnp.bfloat16)


def place_tile(totals, record):
    flux_sums, coverage = totals
    tile_data, target, row_start, col_start, tile_weight = record
    corner = (target, row_start, col_start)
    current = lax.dynamic_slice(flux_sums, corner, (1, S, S))
    flux_sums = lax.dynamic_update_slice(flux_sums, current + tile_data.astype(jnp.float32)[None], corner)
    covered = lax.dynamic_slice(coverage, corner, (1, S, S))
    coverage = lax.dynamic_update_slice(coverage, covered + tile_weight, corner)
    return (flux_sums, coverage), None


def reference(exposures, psf_taps, warp_rows, warp_cols, routes, offsets, weights, det_weight, det_bias):
    per_band = []
    for band_index in range(BANDS):
        warped = warp_band(exposures[:, band_index], psf_taps[:, band_index], warp_rows[:, band_index], warp_cols[:, band_index], weights[band_index])
        start = (jnp.zeros((PATCHES, PS, PS), jnp.float32), jnp.zeros((PATCHES, PS, PS), jnp.float32))
        records = (warped, routes[band_index, :, 0], offsets[band_index, :, 0], offsets[band_index, :, 1], weights[band_index])
        (flux_sums, coverage), unused = lax.scan(place_tile, start, records)
        per_band.append((flux_sums / jnp.maximum(coverage, 1.0)).astype(jnp.bfloat16))
    coadd = jnp.stack(per_band, axis=1)

    def detect_patch(images):
        wide = jnp.pad(images.astype(jnp.float32), ((0, 0), (2, 2), (2, 2)))
        features = jnp.stack([wide[:, row_shift:row_shift + PS, col_shift:col_shift + PS] for row_shift in range(5) for col_shift in range(5)], axis=1)
        features = features.reshape(BANDS * 25, PS * PS)
        result = jnp.dot(det_weight.astype(jnp.float32), features, preferred_element_type=jnp.float32) + det_bias[:, None]
        return result.reshape(CH, PS, PS).astype(jnp.bfloat16)

    detection = lax.map(detect_patch, coadd)
    return coadd, detection
```

```python
import jax
import jax.numpy as jnp
from jax import lax
from jax.experimental import pallas as pl
from jax.experimental.pallas import tpu as pltpu
from jax.sharding import PartitionSpec as P

PS = 512
S = 128
TAPS = 7
HALF = TAPS // 2
KS = 5
PAD = KS // 2
LANES = 128
F32 = jnp.float32
BF16 = jnp.bfloat16


def dot_nt(a, b):
    return lax.dot_general(a, b, (((1,), (1,)), ((), ())), preferred_element_type=F32)


def dot_nn(a, b):
    return lax.dot_general(a, b, (((1,), (0,)), ((), ())), preferred_element_type=F32)


def front_kernel(
    per_step, owner_ref, routes_ref, offs_ref, wts_ref, taps_ref,
    exp_ref, rows_ref, cols_ref, buf0_ref, buf1_ref, extra_ref, stage, count, sems,
):
    step = pl.program_id(0)
    steps = pl.num_programs(0)
    tiles = stage.shape[0]
    base = owner_ref[0] * tiles

    @pl.when(step == 0)
    def _():
        @pl.loop(0, count.shape[0])
        def _(i):
            count[i] = 0

    diag = lax.broadcasted_iota(jnp.int32, (S, S), 1) - lax.broadcasted_iota(jnp.int32, (S, S), 0)
    for k in range(per_step):
        tile = step * per_step + k
        psf_rows = jnp.zeros((S, S), F32)
        psf_cols = jnp.zeros((S, S), F32)
        for tap in range(TAPS):
            on = diag == tap - HALF
            psf_rows = jnp.where(on, taps_ref[tap, tile], psf_rows)
            psf_cols = jnp.where(on, taps_ref[TAPS + tap, tile], psf_cols)
        half_done = dot_nt(exp_ref[k], psf_cols.astype(BF16)).astype(BF16)
        matched = dot_nn(psf_rows.astype(BF16), half_done).astype(BF16)
        across = dot_nt(matched, cols_ref[k]).astype(BF16)
        product = dot_nn(rows_ref[k], across)
        place = base + tile
        warped = wts_ref[0, place] * product
        warped = pltpu.roll(warped, offs_ref[1, place] & (LANES - 1), 1)
        warped = pltpu.roll(warped, offs_ref[0, place] & 7, 0)
        warped = warped.astype(BF16)
        stage[tile] = warped
        dest = routes_ref[0, place]
        rank = count[dest]
        count[dest] = rank + 1

        @pl.when(rank == 0)
        def _():
            pltpu.make_async_copy(stage.at[tile], buf0_ref.at[dest], sems.at[tile]).start()

        @pl.when(rank > 0)
        def _():
            extra_ref[...] = warped
            pltpu.make_async_copy(stage.at[tile], buf1_ref.at[dest], sems.at[tile]).start()

    @pl.when(step == steps - 1)
    def _():
        @pl.loop(0, tiles)
        def _(i):
            pltpu.make_async_copy(stage.at[i], buf0_ref.at[0], sems.at[i]).wait()


def front(owner, routes, offs, wts, taps, exposures, warp_rows, warp_cols, npatch):
    tiles = exposures.shape[0]
    per_step = 4
    spec = pl.BlockSpec((per_step, None, S, S), lambda i, *_: (i, 0, 0, 0))
    anywhere = pl.BlockSpec(memory_space=pl.ANY)
    return pl.pallas_call(
        lambda *refs: front_kernel(per_step, *refs),
        name="front",
        out_shape=(
            jax.ShapeDtypeStruct((npatch, S, S), BF16),
            jax.ShapeDtypeStruct((npatch, S, S), BF16),
            jax.ShapeDtypeStruct((S, S), BF16),
        ),
        grid_spec=pltpu.PrefetchScalarGridSpec(
            num_scalar_prefetch=5,
            grid=(tiles // per_step,),
            in_specs=[spec, spec, spec],
            out_specs=(anywhere, anywhere, pl.BlockSpec((S, S), lambda i, *_: (0, 0))),
            scratch_shapes=[
                pltpu.VMEM((tiles, S, S), BF16),
                pltpu.SMEM((npatch,), jnp.int32),
                pltpu.SemaphoreType.DMA((tiles,)),
            ],
        ),
        compiler_params=pltpu.CompilerParams(
            dimension_semantics=("arbitrary",), vmem_limit_bytes=24 << 20
        ),
    )(owner, routes, offs, wts, taps, exposures, warp_rows, warp_cols)


def place_kernel(per_step, nband, table_ref, first_ref, second_ref, cover_ref, coadd_ref, strip_ref, acc, full):
    step = pl.program_id(0)
    steps = pl.num_programs(0)
    strip_rows = PS // nband
    parts = PS // LANES

    @pl.when(step == 0)
    def _():
        acc[...] = jnp.zeros_like(acc)

    lane = lax.broadcasted_iota(jnp.int32, (8, LANES), 1)
    sub = lax.broadcasted_iota(jnp.int32, (8, LANES), 0)
    for slot, src in ((0, first_ref), (1, second_ref)):
        for k in range(per_step):
            code = table_ref[slot, step * per_step + k]

            @pl.when(code > 0)
            def _():
                corner = code - 1
                top = corner // PS
                left = corner & (PS - 1)
                base = pl.multiple_of((top // 8) * 8, 8)
                shift = top & 7
                part = left // LANES
                on = lane >= (left & (LANES - 1))
                tile = src[k].astype(F32)
                for g in range(S // 8):
                    rows = tile[8 * g : 8 * g + 8]
                    if g == 0:
                        low = jnp.where(sub < shift, rows, 0.0)
                        rows = rows - low
                        at = pl.ds(base + S, 8)
                        acc[part, at, :] += jnp.where(on, low, 0.0)
                        acc[part + 1, at, :] += jnp.where(on, 0.0, low)
                    at = pl.ds(base + 8 * g, 8)
                    acc[part, at, :] += jnp.where(on, rows, 0.0)
                    acc[part + 1, at, :] += jnp.where(on, 0.0, rows)

    @pl.when(step == steps - 1)
    def _():
        edge = full.shape[0] - PS
        full[0 : edge // 2, :] = jnp.zeros((edge // 2, PS), F32)
        full[PS + edge // 2 :, :] = jnp.zeros((edge // 2, PS), F32)
        for part in range(parts):
            at = slice(part * LANES, part * LANES + LANES)
            value = (acc[part, 0:PS, :] / jnp.maximum(cover_ref[:, at], 1.0)).astype(BF16)
            coadd_ref[:, at] = value
            full[edge // 2 : edge // 2 + PS, at] = value.astype(F32)
        for b in range(nband):
            start = edge // 2 - PAD + b * strip_rows
            strip_ref[b] = full[start : start + strip_ref.shape[1], :].astype(BF16)


def place(table, first, second, cover, nband):
    slots = first.shape[0]
    per_step = 8
    strip = PS // nband + 8
    spec = pl.BlockSpec((per_step, S, S), lambda i, *_: (i, 0, 0))
    return pl.pallas_call(
        lambda *refs: place_kernel(per_step, nband, *refs),
        name="place",
        out_shape=(
            jax.ShapeDtypeStruct((PS, PS), BF16),
            jax.ShapeDtypeStruct((nband, strip, PS), BF16),
        ),
        grid_spec=pltpu.PrefetchScalarGridSpec(
            num_scalar_prefetch=1,
            grid=(slots // per_step,),
            in_specs=[spec, spec, pl.BlockSpec((PS, PS), lambda i, *_: (0, 0))],
            out_specs=(
                pl.BlockSpec((PS, PS), lambda i, *_: (0, 0)),
                pl.BlockSpec((nband, strip, PS), lambda i, *_: (0, 0, 0)),
            ),
            scratch_shapes=[
                pltpu.VMEM((PS // LANES + 1, PS + 8, LANES), F32),
                pltpu.VMEM((PS + 16, PS), F32),
            ],
        ),
        compiler_params=pltpu.CompilerParams(
            dimension_semantics=("arbitrary",), vmem_limit_bytes=24 << 20
        ),
    )(table, first, second, cover)


def detect_kernel(nband, strip_ref, weight_ref, bias_ref, out_ref, main, edge):
    step = pl.program_id(0)
    groups = main.shape[0]
    channels = out_ref.shape[0]

    @pl.when(step == 0)
    def _():
        column = lax.broadcasted_iota(jnp.int32, (8, PS), 1)
        for g in range(groups):
            pieces = []
            for s in range(KS):
                for b in range(nband):
                    x = strip_ref[b, 8 * g : 8 * g + 8, :].astype(F32)
                    d = s - PAD
                    if d:
                        x = pltpu.roll(x, (-d) % PS, 1)
                        x = jnp.where((column + d >= 0) & (column + d < PS), x, 0.0)
                    pieces.append(x)
            main[g] = jnp.concatenate(pieces, axis=0).astype(BF16)
            pairs = []
            for i in range(0, len(pieces), 2):
                pairs.append(pieces[i][0:4])
                pairs.append(pieces[i + 1][0:4])
            edge[g] = jnp.concatenate(pairs, axis=0).astype(BF16)

    rhs = jnp.concatenate([main[step], edge[step + 1]], axis=0)
    res = dot_nn(weight_ref[...], rhs) + bias_ref[...]
    out_ref[...] = res.reshape(channels, 8, PS).astype(BF16)


def detect(strips, weight, bias, channels, strip_rows):
    nband, rows, _ = strips.shape
    groups = rows // 8
    depth = nband * KS
    return pl.pallas_call(
        lambda *refs: detect_kernel(nband, *refs),
        name="detect",
        out_shape=jax.ShapeDtypeStruct((channels, strip_rows, PS), BF16),
        grid_spec=pltpu.PrefetchScalarGridSpec(
            num_scalar_prefetch=0,
            grid=(strip_rows // 8,),
            in_specs=[
                pl.BlockSpec(strips.shape, lambda i: (0, 0, 0)),
                pl.BlockSpec(weight.shape, lambda i: (0, 0)),
                pl.BlockSpec(bias.shape, lambda i: (0, 0)),
            ],
            out_specs=pl.BlockSpec((channels, 8, PS), lambda i: (0, i, 0)),
            scratch_shapes=[
                pltpu.VMEM((groups, depth * 8, PS), BF16),
                pltpu.VMEM((groups, depth * 4, PS), BF16),
            ],
        ),
        compiler_params=pltpu.CompilerParams(
            dimension_semantics=("arbitrary",), vmem_limit_bytes=32 << 20
        ),
    )(strips, weight, bias)


def toeplitz(det_weight, nband):
    channels = det_weight.shape[0]
    taps = det_weight.reshape(channels, nband, KS, KS).transpose(0, 3, 1, 2)
    row_out = jnp.arange(8)[:, None]
    out = []
    for lo, hi in ((0, 8), (8, 12)):
        row_in = jnp.arange(lo, hi)[None, :]
        total = jnp.zeros((channels, 8, KS, nband, hi - lo), det_weight.dtype)
        for r in range(KS):
            on = (row_in - row_out == r)[None, :, None, None, :]
            total = jnp.where(on, taps[:, None, :, :, r, None], total)
        out.append(total.reshape(channels * 8, KS * nband * (hi - lo)))
    return jnp.concatenate(out, axis=1)


def slot_select(targets, capacity):
    counts = jnp.cumsum(targets.astype(jnp.int32), axis=1) - 1
    slot_ids = jnp.arange(capacity, dtype=jnp.int32)
    return targets[None] & (counts[None] == slot_ids[:, None, None])


def body(exposures, psf_taps, warp_rows, warp_cols, routes, offsets, weights, det_weight, det_bias):
    npatch = lax.axis_size("patch")
    nband = lax.axis_size("band")
    tiles = exposures.shape[0]
    capacity = 2
    owner = lax.axis_index("patch").astype(jnp.int32)
    routes_row = routes.transpose(0, 2, 1).reshape(1, -1)
    offs_rows = offsets.transpose(0, 2, 1).reshape(2, -1)
    taps = psf_taps[:, 0].transpose(1, 2, 0).reshape(2 * TAPS, tiles).astype(F32)
    buf0, buf1, extra = front(
        owner[None], routes_row, offs_rows, weights, taps, exposures, warp_rows, warp_cols, npatch
    )
    dest_all = routes_row.reshape(npatch, tiles)
    same = (dest_all[:, :, None] == dest_all[:, None, :]) & (
        jnp.arange(tiles)[None, :, None] > jnp.arange(tiles)[None, None, :]
    )
    repeats = jnp.max(jnp.sum(jnp.any(same, axis=2).astype(F32), axis=1))
    repeats = lax.pmax(repeats, "band")
    first = lax.all_to_all(buf0, "patch", split_axis=0, concat_axis=0, tiled=True)
    second = lax.cond(
        repeats <= 1.0,
        lambda: lax.all_gather(extra, "patch"),
        lambda: lax.all_to_all(buf1, "patch", split_axis=0, concat_axis=0, tiled=True),
    )
    landed = slot_select(dest_all == owner, capacity)
    corner = (offs_rows[0] * PS + offs_rows[1] + 1).reshape(npatch, tiles)
    table = jnp.sum(jnp.where(landed, corner[None], 0), axis=-1)
    slot_weights = jnp.sum(
        jnp.where(landed, weights.reshape(npatch, tiles)[None], 0.0), axis=-1
    ).reshape(-1)
    slot_corner = jnp.maximum(table.reshape(-1) - 1, 0)
    pixels = jnp.arange(PS, dtype=jnp.int32)
    down = pixels[None, :] - (slot_corner // PS)[:, None]
    right = pixels[None, :] - (slot_corner % PS)[:, None]
    row_cover = jnp.where((down >= 0) & (down < S), slot_weights[:, None], 0.0)
    col_cover = ((right >= 0) & (right < S)).astype(F32)
    cover = jnp.einsum("ky,kx->yx", row_cover, col_cover, precision=lax.Precision.HIGHEST)
    coadd, strips = place(table, first, second, cover, nband)
    strips = lax.all_to_all(strips, "band", split_axis=0, concat_axis=0, tiled=True)
    channels = det_weight.shape[0]
    strip_rows = PS // nband
    bias = jnp.broadcast_to(det_bias[:, None, None], (channels, 8, 1)).reshape(channels * 8, 1)
    detection = detect(strips, toeplitz(det_weight, nband), bias, channels, strip_rows)
    return (coadd[None, None], detection[None])


def solution(mesh):
    placed = (
        P("patch", "band", None, None),
        P("patch", "band", None, None),
        P("patch", "band", None, None),
        P("patch", "band", None, None),
        P("band", None, None),
        P("band", None, None),
        P("band", None),
        P(),
        P(),
    )
    return jax.shard_map(
        body,
        mesh=mesh,
        in_specs=placed,
        out_specs=(P("patch", "band", None, None), P("patch", None, "band", None)),
        check_vma=False,
    )
```

```python
import jax
import jax.numpy as jnp
from jax import lax
from jax.experimental import pallas as pl
from jax.experimental.pallas import tpu as pltpu
from jax.sharding import PartitionSpec as P

PS = 512
S = 128
TAPS = 7
HALF = TAPS // 2
KS = 5
PAD = KS // 2
LANES = 128
F32 = jnp.float32
BF16 = jnp.bfloat16


def dot_nt(a, b):
    return lax.dot_general(a, b, (((1,), (1,)), ((), ())), preferred_element_type=F32)


def dot_nn(a, b):
    return lax.dot_general(a, b, (((1,), (0,)), ((), ())), preferred_element_type=F32)


def front_kernel(
    per_step, owner_ref, routes_ref, offs_ref, wts_ref, taps_ref,
    exp_ref, rows_ref, cols_ref, buf0_ref, buf1_ref, extra_ref, stage, count, sems,
):
    step = pl.program_id(0)
    steps = pl.num_programs(0)
    tiles = stage.shape[0]
    base = owner_ref[0] * tiles

    @pl.when(step == 0)
    def _():
        @pl.loop(0, count.shape[0])
        def _(i):
            count[i] = 0

    diag = lax.broadcasted_iota(jnp.int32, (S, S), 1) - lax.broadcasted_iota(jnp.int32, (S, S), 0)

    def band(first_tap, tile):
        matrix = jnp.zeros((S, S), F32)
        for tap in range(TAPS):
            matrix = jnp.where(diag == tap - HALF, taps_ref[first_tap + tap, tile], matrix)
        return matrix.astype(BF16)

    each = range(per_step)
    here = [step * per_step + k for k in each]
    psf_rows = [band(0, t) for t in here]
    psf_cols = [band(TAPS, t) for t in here]
    half_done = [dot_nt(exp_ref[k], psf_cols[k]).astype(BF16) for k in each]
    matched = [dot_nn(psf_rows[k], half_done[k]).astype(BF16) for k in each]
    across = [dot_nt(matched[k], cols_ref[k]).astype(BF16) for k in each]
    product = [dot_nn(rows_ref[k], across[k]) for k in each]
    for k in each:
        place = base + here[k]
        warped = wts_ref[0, place] * product[k]
        warped = pltpu.roll(warped, offs_ref[1, place] & (LANES - 1), 1)
        warped = pltpu.roll(warped, offs_ref[0, place] & 7, 0)
        stage[here[k]] = warped.astype(BF16)
    for k in each:
        dest = routes_ref[0, base + here[k]]
        rank = count[dest]
        count[dest] = rank + 1

        @pl.when(rank == 0)
        def _():
            pltpu.make_async_copy(stage.at[here[k]], buf0_ref.at[dest], sems.at[here[k]]).start()

        @pl.when(rank > 0)
        def _():
            extra_ref[...] = stage[here[k]]
            pltpu.make_async_copy(stage.at[here[k]], buf1_ref.at[dest], sems.at[here[k]]).start()

    @pl.when(step == steps - 1)
    def _():
        @pl.loop(0, tiles)
        def _(i):
            pltpu.make_async_copy(stage.at[i], buf0_ref.at[0], sems.at[i]).wait()


def front(owner, routes, offs, wts, taps, exposures, warp_rows, warp_cols, npatch):
    tiles = exposures.shape[0]
    per_step = 16
    spec = pl.BlockSpec((per_step, None, S, S), lambda i, *_: (i, 0, 0, 0))
    anywhere = pl.BlockSpec(memory_space=pl.ANY)
    return pl.pallas_call(
        lambda *refs: front_kernel(per_step, *refs),
        name="front",
        out_shape=(
            jax.ShapeDtypeStruct((npatch, S, S), BF16),
            jax.ShapeDtypeStruct((npatch, S, S), BF16),
            jax.ShapeDtypeStruct((S, S), BF16),
        ),
        grid_spec=pltpu.PrefetchScalarGridSpec(
            num_scalar_prefetch=5,
            grid=(tiles // per_step,),
            in_specs=[spec, spec, spec],
            out_specs=(anywhere, anywhere, pl.BlockSpec((S, S), lambda i, *_: (0, 0))),
            scratch_shapes=[
                pltpu.VMEM((tiles, S, S), BF16),
                pltpu.SMEM((npatch,), jnp.int32),
                pltpu.SemaphoreType.DMA((tiles,)),
            ],
        ),
        compiler_params=pltpu.CompilerParams(
            dimension_semantics=("arbitrary",)
        ),
    )(owner, routes, offs, wts, taps, exposures, warp_rows, warp_cols)


def spread(index, masks):
    total = 0
    for bit, mask in enumerate(masks):
        total = total | (((index >> bit) & 1) * mask)
    return total


def swap(x, axis, mask):
    size = lax.axis_size(axis)
    return lax.ppermute(x, axis, [(i, i ^ mask) for i in range(size)])


def place_kernel(per_step, nband, masks, owner_ref, table_ref, first_ref, second_ref, cover_ref, coadd_ref, strip_ref, acc, full):
    step = pl.program_id(0)
    steps = pl.num_programs(0)
    strip_rows = PS // nband
    parts = PS // LANES

    @pl.when(step == 0)
    def _():
        acc[...] = jnp.zeros_like(acc)

    lane = lax.broadcasted_iota(jnp.int32, (8, LANES), 1)
    sub = lax.broadcasted_iota(jnp.int32, (8, LANES), 0)
    for slot, src in ((0, first_ref), (1, second_ref)):
        for k in range(per_step):
            source = step * per_step + k
            if slot == 1 and masks:
                source = owner_ref[0] ^ spread(source, masks)
            code = table_ref[slot, source]

            @pl.when(code > 0)
            def _():
                corner = code - 1
                top = corner // PS
                left = corner & (PS - 1)
                base = pl.multiple_of((top // 8) * 8, 8)
                shift = top & 7
                part = left // LANES
                on = lane >= (left & (LANES - 1))
                tile = src[k].astype(F32)
                for g in range(S // 8):
                    rows = tile[8 * g : 8 * g + 8]
                    if g == 0:
                        low = jnp.where(sub < shift, rows, 0.0)
                        rows = rows - low
                        at = pl.ds(base + S, 8)
                        acc[part, at, :] += jnp.where(on, low, 0.0)
                        acc[part + 1, at, :] += jnp.where(on, 0.0, low)
                    at = pl.ds(base + 8 * g, 8)
                    acc[part, at, :] += jnp.where(on, rows, 0.0)
                    acc[part + 1, at, :] += jnp.where(on, 0.0, rows)

    @pl.when(step == steps - 1)
    def _():
        edge = full.shape[0] - PS
        full[0 : edge // 2, :] = jnp.zeros((edge // 2, PS), F32)
        full[PS + edge // 2 :, :] = jnp.zeros((edge // 2, PS), F32)
        for part in range(parts):
            at = slice(part * LANES, part * LANES + LANES)
            value = (acc[part, 0:PS, :] / jnp.maximum(cover_ref[:, at], 1.0)).astype(BF16)
            coadd_ref[:, at] = value
            full[edge // 2 : edge // 2 + PS, at] = value.astype(F32)
        for b in range(nband):
            start = edge // 2 - PAD + b * strip_rows
            strip_ref[b] = full[start : start + strip_ref.shape[1], :].astype(BF16)


def place(owner, table, first, second, cover, nband, masks):
    slots = first.shape[0]
    per_step = 16
    strip = PS // nband + 8
    spec = pl.BlockSpec((per_step, S, S), lambda i, *_: (i, 0, 0))
    return pl.pallas_call(
        lambda *refs: place_kernel(per_step, nband, masks, *refs),
        name="place",
        out_shape=(
            jax.ShapeDtypeStruct((PS, PS), BF16),
            jax.ShapeDtypeStruct((nband, strip, PS), BF16),
        ),
        grid_spec=pltpu.PrefetchScalarGridSpec(
            num_scalar_prefetch=2,
            grid=(slots // per_step,),
            in_specs=[spec, spec, pl.BlockSpec((PS, PS), lambda i, *_: (0, 0))],
            out_specs=(
                pl.BlockSpec((PS, PS), lambda i, *_: (0, 0)),
                pl.BlockSpec((nband, strip, PS), lambda i, *_: (0, 0, 0)),
            ),
            scratch_shapes=[
                pltpu.VMEM((PS // LANES + 1, PS + 8, LANES), F32),
                pltpu.VMEM((PS + 16, PS), F32),
            ],
        ),
        compiler_params=pltpu.CompilerParams(
            dimension_semantics=("arbitrary",)
        ),
    )(owner, table, first, second, cover)


def detect_kernel(nband, strip_ref, weight_ref, bias_ref, out_ref, main, edge):
    step = pl.program_id(0)
    groups = main.shape[0]
    channels = out_ref.shape[0]

    @pl.when(step == 0)
    def _():
        column = lax.broadcasted_iota(jnp.int32, (8, PS), 1)
        for g in range(groups):
            pieces = []
            for s in range(KS):
                for b in range(nband):
                    x = strip_ref[b, 8 * g : 8 * g + 8, :].astype(F32)
                    d = s - PAD
                    if d:
                        x = pltpu.roll(x, (-d) % PS, 1)
                        x = jnp.where((column + d >= 0) & (column + d < PS), x, 0.0)
                    pieces.append(x)
            main[g] = jnp.concatenate(pieces, axis=0).astype(BF16)
            pairs = []
            for i in range(0, len(pieces), 2):
                pairs.append(pieces[i][0:4])
                pairs.append(pieces[i + 1][0:4])
            edge[g] = jnp.concatenate(pairs, axis=0).astype(BF16)

    per_step = out_ref.shape[1] // 8
    for i in range(per_step):
        g = step * per_step + i
        rhs = jnp.concatenate([main[g], edge[g + 1]], axis=0)
        res = dot_nn(weight_ref[...], rhs) + bias_ref[...]
        out_ref[:, 8 * i : 8 * i + 8, :] = res.reshape(channels, 8, PS).astype(BF16)


def detect(strips, weight, bias, channels, strip_rows):
    nband, rows, _ = strips.shape
    groups = rows // 8
    depth = nband * KS
    step_rows = 32
    return pl.pallas_call(
        lambda *refs: detect_kernel(nband, *refs),
        name="detect",
        out_shape=jax.ShapeDtypeStruct((channels, strip_rows, PS), BF16),
        grid_spec=pltpu.PrefetchScalarGridSpec(
            num_scalar_prefetch=0,
            grid=(strip_rows // step_rows,),
            in_specs=[
                pl.BlockSpec(strips.shape, lambda i: (0, 0, 0)),
                pl.BlockSpec(weight.shape, lambda i: (0, 0)),
                pl.BlockSpec(bias.shape, lambda i: (0, 0)),
            ],
            out_specs=pl.BlockSpec((channels, step_rows, PS), lambda i: (0, i, 0)),
            scratch_shapes=[
                pltpu.VMEM((groups, depth * 8, PS), BF16),
                pltpu.VMEM((groups, depth * 4, PS), BF16),
            ],
        ),
        compiler_params=pltpu.CompilerParams(
            dimension_semantics=("arbitrary",)
        ),
    )(strips, weight, bias)


def toeplitz(det_weight, nband):
    channels = det_weight.shape[0]
    taps = det_weight.reshape(channels, nband, KS, KS).transpose(0, 3, 1, 2)
    row_out = jnp.arange(8)[:, None]
    out = []
    for lo, hi in ((0, 8), (8, 12)):
        row_in = jnp.arange(lo, hi)[None, :]
        total = jnp.zeros((channels, 8, KS, nband, hi - lo), det_weight.dtype)
        for r in range(KS):
            on = (row_in - row_out == r)[None, :, None, None, :]
            total = jnp.where(on, taps[:, None, :, :, r, None], total)
        out.append(total.reshape(channels * 8, KS * nband * (hi - lo)))
    return jnp.concatenate(out, axis=1)


def slot_select(targets, capacity):
    counts = jnp.cumsum(targets.astype(jnp.int32), axis=1) - 1
    slot_ids = jnp.arange(capacity, dtype=jnp.int32)
    return targets[None] & (counts[None] == slot_ids[:, None, None])


def body(exposures, psf_taps, warp_rows, warp_cols, routes, offsets, weights, det_weight, det_bias):
    npatch = lax.axis_size("patch")
    nband = lax.axis_size("band")
    tiles = exposures.shape[0]
    capacity = 2
    owner = lax.axis_index("patch").astype(jnp.int32)
    routes_row = routes.transpose(0, 2, 1).reshape(1, -1)
    offs_rows = offsets.transpose(0, 2, 1).reshape(2, -1)
    taps = psf_taps[:, 0].transpose(1, 2, 0).reshape(2 * TAPS, tiles).astype(F32)
    buf0, buf1, extra = front(
        owner[None], routes_row, offs_rows, weights, taps, exposures, warp_rows, warp_cols, npatch
    )
    first = lax.all_to_all(buf0, "patch", split_axis=0, concat_axis=0, tiled=True)
    bits = npatch.bit_length() - 1
    masks = [1 << bit for bit in [*range(3, bits), 1, 2, 0] if bit < bits]
    second = extra[None]
    for mask in masks:
        second = jnp.concatenate([second, swap(second, "patch", mask)], axis=0)
    dest_all = routes_row.reshape(npatch, tiles)
    same = (dest_all[:, :, None] == dest_all[:, None, :]) & (
        jnp.arange(tiles)[None, :, None] > jnp.arange(tiles)[None, None, :]
    )
    repeats = jnp.max(jnp.sum(jnp.any(same, axis=2).astype(F32), axis=1))
    for bit in range(nband.bit_length() - 1):
        repeats = jnp.maximum(repeats, swap(repeats, "band", 1 << bit))
    landed = slot_select(dest_all == owner, capacity)
    corner = (offs_rows[0] * PS + offs_rows[1] + 1).reshape(npatch, tiles)
    table = jnp.sum(jnp.where(landed, corner[None], 0), axis=-1)
    slot_weights = jnp.sum(
        jnp.where(landed, weights.reshape(npatch, tiles)[None], 0.0), axis=-1
    ).reshape(-1)
    slot_corner = jnp.maximum(table.reshape(-1) - 1, 0)
    pixels = jnp.arange(PS, dtype=jnp.int32)
    down = pixels[None, :] - (slot_corner // PS)[:, None]
    right = pixels[None, :] - (slot_corner % PS)[:, None]
    row_cover = jnp.where((down >= 0) & (down < S), slot_weights[:, None], 0.0)
    col_cover = ((right >= 0) & (right < S)).astype(F32)
    cover = jnp.einsum("ky,kx->yx", row_cover, col_cover, precision=lax.Precision.HIGHEST)
    channels = det_weight.shape[0]
    strip_rows = PS // nband
    bias = jnp.broadcast_to(det_bias[:, None, None], (channels, 8, 1)).reshape(channels * 8, 1)
    first, second, table, cover, kernel, bias, repeats = lax.optimization_barrier(
        (first, second, table, cover, toeplitz(det_weight, nband), bias, repeats)
    )

    def one_repeat():
        return place(owner[None], table, first, second, cover, nband, masks)

    def any_repeats():
        rest = lax.all_to_all(buf1, "patch", split_axis=0, concat_axis=0, tiled=True)
        return place(owner[None], table, first, rest, cover, nband, None)

    coadd, strips = lax.cond(repeats <= 1.0, one_repeat, any_repeats)
    strips = lax.all_to_all(strips, "band", split_axis=0, concat_axis=0, tiled=True)
    detection = detect(strips, kernel, bias, channels, strip_rows)
    return (coadd[None, None], detection[None])


def solution(mesh):
    placed = (
        P("patch", "band", None, None),
        P("patch", "band", None, None),
        P("patch", "band", None, None),
        P("patch", "band", None, None),
        P("band", None, None),
        P("band", None, None),
        P("band", None),
        P(),
        P(),
    )
    return jax.shard_map(
        body,
        mesh=mesh,
        in_specs=placed,
        out_specs=(P("patch", "band", None, None), P("patch", None, "band", None)),
        check_vma=False,
    )
```

```python
import jax
import jax.numpy as jnp
from jax import lax
from jax.experimental import pallas as pl
from jax.experimental.pallas import tpu as pltpu
from jax.sharding import PartitionSpec as P

PS = 512
S = 128
TAPS = 7
HALF = TAPS // 2
KS = 5
PAD = KS // 2
LANES = 128
F32 = jnp.float32
BF16 = jnp.bfloat16


def dot_nt(a, b):
    return lax.dot_general(a, b, (((1,), (1,)), ((), ())), preferred_element_type=F32)


def dot_nn(a, b):
    return lax.dot_general(a, b, (((1,), (0,)), ((), ())), preferred_element_type=F32)


def warp_tiles(here, base, offs_ref, wts_ref, taps_ref, tiles, rows, cols):
    diag = lax.broadcasted_iota(jnp.int32, (S, S), 1) - lax.broadcasted_iota(jnp.int32, (S, S), 0)

    def band(first_tap, tile):
        matrix = jnp.zeros((S, S), F32)
        for tap in range(TAPS):
            matrix = jnp.where(diag == tap - HALF, taps_ref[first_tap + tap, tile], matrix)
        return matrix.astype(BF16)

    each = range(len(here))
    psf_rows = [band(0, t) for t in here]
    psf_cols = [band(TAPS, t) for t in here]
    half_done = [dot_nt(tiles[k], psf_cols[k]).astype(BF16) for k in each]
    matched = [dot_nn(psf_rows[k], half_done[k]).astype(BF16) for k in each]
    across = [dot_nt(matched[k], cols[k]).astype(BF16) for k in each]
    product = [dot_nn(rows[k], across[k]) for k in each]
    out = []
    for k in each:
        place = base + here[k]
        warped = wts_ref[0, place] * product[k]
        warped = pltpu.roll(warped, offs_ref[1, place] & (LANES - 1), 1)
        warped = pltpu.roll(warped, offs_ref[0, place] & 7, 0)
        out.append(warped.astype(BF16))
    return out


def repeat_kernel(
    tiles, owner_ref, routes_ref, offs_ref, wts_ref, taps_ref,
    exp_ref, rows_ref, cols_ref, out_ref, held, count, found, sems,
):
    base = owner_ref[0] * tiles
    found[0] = 0

    @pl.loop(0, count.shape[0])
    def _(i):
        count[i] = 0

    @pl.loop(0, tiles)
    def _(i):
        dest = routes_ref[0, base + i]
        rank = count[dest]
        count[dest] = rank + 1
        found[0] = jnp.where(rank > 0, i, found[0])

    tile = found[0]
    copies = [
        pltpu.make_async_copy(src.at[tile, 0], held.at[i], sems.at[i])
        for i, src in enumerate((exp_ref, rows_ref, cols_ref))
    ]
    for copy in copies:
        copy.start()
    for copy in copies:
        copy.wait()
    out_ref[0] = warp_tiles(
        [tile], base, offs_ref, wts_ref, taps_ref, [held[0]], [held[1]], [held[2]]
    )[0]


def repeat(owner, routes, offs, wts, taps, exposures, warp_rows, warp_cols, npatch):
    anywhere = pl.BlockSpec(memory_space=pl.ANY)
    return pl.pallas_call(
        lambda *refs: repeat_kernel(exposures.shape[0], *refs),
        name="repeat",
        out_shape=jax.ShapeDtypeStruct((1, S, S), BF16),
        grid_spec=pltpu.PrefetchScalarGridSpec(
            num_scalar_prefetch=5,
            grid=(1,),
            in_specs=[anywhere] * 3,
            out_specs=pl.BlockSpec((1, S, S), lambda i, *_: (0, 0, 0)),
            scratch_shapes=[
                pltpu.VMEM((3, S, S), BF16),
                pltpu.SMEM((npatch,), jnp.int32),
                pltpu.SMEM((1,), jnp.int32),
                pltpu.SemaphoreType.DMA((3,)),
            ],
        ),
    )(owner, routes, offs, wts, taps, exposures, warp_rows, warp_cols)


def front_kernel(
    per_step, owner_ref, routes_ref, offs_ref, wts_ref, taps_ref,
    exp_ref, rows_ref, cols_ref, buf0_ref, buf1_ref, stage, count, sems,
):
    step = pl.program_id(0)
    steps = pl.num_programs(0)
    tiles = stage.shape[0]
    base = owner_ref[0] * tiles

    @pl.when(step == 0)
    def _():
        @pl.loop(0, count.shape[0])
        def _(i):
            count[i] = 0

    here = [step * per_step + k for k in range(per_step)]
    inputs = [[ref[k] for k in range(per_step)] for ref in (exp_ref, rows_ref, cols_ref)]
    warped = warp_tiles(here, base, offs_ref, wts_ref, taps_ref, *inputs)
    for tile, value in zip(here, warped):
        stage[tile] = value
    for tile in here:
        dest = routes_ref[0, base + tile]
        rank = count[dest]
        count[dest] = rank + 1

        @pl.when(rank == 0)
        def _():
            pltpu.make_async_copy(stage.at[tile], buf0_ref.at[dest], sems.at[tile]).start()

        @pl.when(rank > 0)
        def _():
            pltpu.make_async_copy(stage.at[tile], buf1_ref.at[dest], sems.at[tile]).start()

    @pl.when(step == steps - 1)
    def _():
        @pl.loop(0, tiles)
        def _(i):
            pltpu.make_async_copy(stage.at[i], buf0_ref.at[0], sems.at[i]).wait()


def front(owner, routes, offs, wts, taps, exposures, warp_rows, warp_cols, npatch):
    tiles = exposures.shape[0]
    per_step = 16
    spec = pl.BlockSpec((per_step, None, S, S), lambda i, *_: (i, 0, 0, 0))
    anywhere = pl.BlockSpec(memory_space=pl.ANY)
    return pl.pallas_call(
        lambda *refs: front_kernel(per_step, *refs),
        name="front",
        out_shape=(
            jax.ShapeDtypeStruct((npatch, S, S), BF16),
            jax.ShapeDtypeStruct((npatch, S, S), BF16),
        ),
        cost_estimate=pl.CostEstimate(flops=0, bytes_accessed=24 << 20, transcendentals=0),
        grid_spec=pltpu.PrefetchScalarGridSpec(
            num_scalar_prefetch=5,
            grid=(tiles // per_step,),
            in_specs=[spec, spec, spec],
            out_specs=(anywhere, anywhere),
            scratch_shapes=[
                pltpu.VMEM((tiles, S, S), BF16),
                pltpu.SMEM((npatch,), jnp.int32),
                pltpu.SemaphoreType.DMA((tiles,)),
            ],
        ),
        compiler_params=pltpu.CompilerParams(
            dimension_semantics=("arbitrary",)
        ),
    )(owner, routes, offs, wts, taps, exposures, warp_rows, warp_cols)


def spread(index, masks):
    total = 0
    for bit, mask in enumerate(masks):
        total = total | (((index >> bit) & 1) * mask)
    return total


def swap(x, axis, mask):
    size = lax.axis_size(axis)
    return lax.ppermute(x, axis, [(i, i ^ mask) for i in range(size)])


def place_kernel(per_step, nband, masks, owner_ref, table_ref, first_ref, *refs):
    *second_refs, cover_ref, coadd_ref, strip_ref, acc, full = refs
    step = pl.program_id(0)
    steps = pl.num_programs(0)
    strip_rows = PS // nband
    parts = PS // LANES

    @pl.when(step == 0)
    def _():
        acc[...] = jnp.zeros_like(acc)

    lane = lax.broadcasted_iota(jnp.int32, (8, LANES), 1)
    sub = lax.broadcasted_iota(jnp.int32, (8, LANES), 0)
    for slot, src in ((0, first_ref), *((1 + i, ref) for i, ref in enumerate(second_refs))):
        for k in range(src.shape[0]):
            source = step * src.shape[0] + k
            if slot > 1:
                source = source + (slot - 1) * src.shape[0] * steps
            if slot and masks:
                source = owner_ref[0] ^ spread(source, masks)
            code = table_ref[min(slot, 1), source]

            @pl.when(code > 0)
            def _():
                corner = code - 1
                top = corner // PS
                left = corner & (PS - 1)
                base = pl.multiple_of((top // 8) * 8, 8)
                shift = top & 7
                part = left // LANES
                on = lane >= (left & (LANES - 1))
                tile = src[k].astype(F32)
                for g in range(S // 8):
                    rows = tile[8 * g : 8 * g + 8]
                    if g == 0:
                        low = jnp.where(sub < shift, rows, 0.0)
                        rows = rows - low
                        at = pl.ds(base + S, 8)
                        acc[part, at, :] += jnp.where(on, low, 0.0)
                        acc[part + 1, at, :] += jnp.where(on, 0.0, low)
                    at = pl.ds(base + 8 * g, 8)
                    acc[part, at, :] += jnp.where(on, rows, 0.0)
                    acc[part + 1, at, :] += jnp.where(on, 0.0, rows)

    @pl.when(step == steps - 1)
    def _():
        edge = full.shape[0] - PS
        full[0 : edge // 2, :] = jnp.zeros((edge // 2, PS), F32)
        full[PS + edge // 2 :, :] = jnp.zeros((edge // 2, PS), F32)
        for part in range(parts):
            at = slice(part * LANES, part * LANES + LANES)
            value = (acc[part, 0:PS, :] / jnp.maximum(cover_ref[:, at], 1.0)).astype(BF16)
            coadd_ref[:, at] = value
            full[edge // 2 : edge // 2 + PS, at] = value.astype(F32)
        for b in range(nband):
            start = edge // 2 - PAD + b * strip_rows
            strip_ref[b] = full[start : start + strip_ref.shape[1], :].astype(BF16)


def place(owner, table, first, seconds, cover, nband, masks):
    per_step = 16
    steps = first.shape[0] // per_step
    strip = PS // nband + 8
    specs = [
        pl.BlockSpec((x.shape[0] // steps, S, S), lambda i, *_: (i, 0, 0)) for x in (first, *seconds)
    ]
    return pl.pallas_call(
        lambda *refs: place_kernel(per_step, nband, masks, *refs),
        name="place",
        out_shape=(
            jax.ShapeDtypeStruct((PS, PS), BF16),
            jax.ShapeDtypeStruct((nband, strip, PS), BF16),
        ),
        grid_spec=pltpu.PrefetchScalarGridSpec(
            num_scalar_prefetch=2,
            grid=(steps,),
            in_specs=[*specs, pl.BlockSpec((PS, PS), lambda i, *_: (0, 0))],
            out_specs=(
                pl.BlockSpec((PS, PS), lambda i, *_: (0, 0)),
                pl.BlockSpec((nband, strip, PS), lambda i, *_: (0, 0, 0)),
            ),
            scratch_shapes=[
                pltpu.VMEM((PS // LANES + 1, PS + 8, LANES), F32),
                pltpu.VMEM((PS + 16, PS), F32),
            ],
        ),
        compiler_params=pltpu.CompilerParams(
            dimension_semantics=("arbitrary",)
        ),
    )(owner, table, first, *seconds, cover)


def detect_kernel(nband, strip_ref, weight_ref, bias_ref, out_ref, main, edge):
    step = pl.program_id(0)
    groups = main.shape[0]
    channels = out_ref.shape[0]

    @pl.when(step == 0)
    def _():
        column = lax.broadcasted_iota(jnp.int32, (8, PS), 1)
        for g in range(groups):
            pieces = []
            for s in range(KS):
                for b in range(nband):
                    x = strip_ref[b, 8 * g : 8 * g + 8, :].astype(F32)
                    d = s - PAD
                    if d:
                        x = pltpu.roll(x, (-d) % PS, 1)
                        x = jnp.where((column + d >= 0) & (column + d < PS), x, 0.0)
                    pieces.append(x)
            main[g] = jnp.concatenate(pieces, axis=0).astype(BF16)
            pairs = []
            for i in range(0, len(pieces), 2):
                pairs.append(pieces[i][0:4])
                pairs.append(pieces[i + 1][0:4])
            edge[g] = jnp.concatenate(pairs, axis=0).astype(BF16)

    per_step = out_ref.shape[1] // 8
    for i in range(per_step):
        g = step * per_step + i
        rhs = jnp.concatenate([main[g], edge[g + 1]], axis=0)
        res = dot_nn(weight_ref[...], rhs) + bias_ref[...]
        out_ref[:, 8 * i : 8 * i + 8, :] = res.reshape(channels, 8, PS).astype(BF16)


def detect(strips, weight, bias, channels, strip_rows):
    nband, rows, _ = strips.shape
    groups = rows // 8
    depth = nband * KS
    step_rows = 32
    return pl.pallas_call(
        lambda *refs: detect_kernel(nband, *refs),
        name="detect",
        out_shape=jax.ShapeDtypeStruct((channels, strip_rows, PS), BF16),
        grid_spec=pltpu.PrefetchScalarGridSpec(
            num_scalar_prefetch=0,
            grid=(strip_rows // step_rows,),
            in_specs=[
                pl.BlockSpec(strips.shape, lambda i: (0, 0, 0)),
                pl.BlockSpec(weight.shape, lambda i: (0, 0)),
                pl.BlockSpec(bias.shape, lambda i: (0, 0)),
            ],
            out_specs=pl.BlockSpec((channels, step_rows, PS), lambda i: (0, i, 0)),
            scratch_shapes=[
                pltpu.VMEM((groups, depth * 8, PS), BF16),
                pltpu.VMEM((groups, depth * 4, PS), BF16),
            ],
        ),
        compiler_params=pltpu.CompilerParams(
            dimension_semantics=("arbitrary",)
        ),
    )(strips, weight, bias)


def toeplitz(det_weight, nband):
    channels = det_weight.shape[0]
    taps = det_weight.reshape(channels, nband, KS, KS).transpose(0, 3, 1, 2)
    row_out = jnp.arange(8)[:, None]
    out = []
    for lo, hi in ((0, 8), (8, 12)):
        row_in = jnp.arange(lo, hi)[None, :]
        total = jnp.zeros((channels, 8, KS, nband, hi - lo), det_weight.dtype)
        for r in range(KS):
            on = (row_in - row_out == r)[None, :, None, None, :]
            total = jnp.where(on, taps[:, None, :, :, r, None], total)
        out.append(total.reshape(channels * 8, KS * nband * (hi - lo)))
    return jnp.concatenate(out, axis=1)


def slot_select(targets, capacity):
    counts = jnp.cumsum(targets.astype(jnp.int32), axis=1) - 1
    slot_ids = jnp.arange(capacity, dtype=jnp.int32)
    return targets[None] & (counts[None] == slot_ids[:, None, None])


def body(exposures, psf_taps, warp_rows, warp_cols, routes, offsets, weights, det_weight, det_bias):
    npatch = lax.axis_size("patch")
    nband = lax.axis_size("band")
    tiles = exposures.shape[0]
    capacity = 2
    owner = lax.axis_index("patch").astype(jnp.int32)
    routes_row = routes.transpose(0, 2, 1).reshape(1, -1)
    offs_rows = offsets.transpose(0, 2, 1).reshape(2, -1)
    taps = psf_taps[:, 0].transpose(1, 2, 0).reshape(2 * TAPS, tiles).astype(F32)
    inputs = (owner[None], routes_row, offs_rows, weights, taps, exposures, warp_rows, warp_cols)
    near = repeat(*inputs, npatch)
    bits = npatch.bit_length() - 1
    masks = [1 << bit for bit in [*range(3, bits), 1, 2, 0] if bit < bits]
    for mask in masks[:-3]:
        near = jnp.concatenate([near, swap(near, "patch", mask)], axis=0)
    buf0, buf1 = front(*inputs, npatch)
    buf0, near = lax.optimization_barrier((buf0, near))
    near = jnp.concatenate([near] + [swap(near, "patch", m) for m in (2, 4, 6)], axis=0)
    first = lax.all_to_all(buf0, "patch", split_axis=0, concat_axis=0, tiled=True)
    dest_all = routes_row.reshape(npatch, tiles)
    same = (dest_all[:, :, None] == dest_all[:, None, :]) & (
        jnp.arange(tiles)[None, :, None] > jnp.arange(tiles)[None, None, :]
    )
    repeats = jnp.max(jnp.sum(jnp.any(same, axis=2).astype(F32), axis=1))
    for bit in range(nband.bit_length() - 1):
        repeats = jnp.maximum(repeats, swap(repeats, "band", 1 << bit))
    landed = slot_select(dest_all == owner, capacity)
    corner = (offs_rows[0] * PS + offs_rows[1] + 1).reshape(npatch, tiles)
    table = jnp.sum(jnp.where(landed, corner[None], 0), axis=-1)
    slot_weights = jnp.sum(
        jnp.where(landed, weights.reshape(npatch, tiles)[None], 0.0), axis=-1
    ).reshape(-1)
    slot_corner = jnp.maximum(table.reshape(-1) - 1, 0)
    pixels = jnp.arange(PS, dtype=jnp.int32)
    down = pixels[None, :] - (slot_corner // PS)[:, None]
    right = pixels[None, :] - (slot_corner % PS)[:, None]
    row_cover = jnp.where((down >= 0) & (down < S), slot_weights[:, None], 0.0)
    col_cover = ((right >= 0) & (right < S)).astype(F32)
    cover = jnp.einsum("ky,kx->yx", row_cover, col_cover, precision=lax.Precision.HIGHEST)
    channels = det_weight.shape[0]
    strip_rows = PS // nband
    bias = jnp.broadcast_to(det_bias[:, None, None], (channels, 8, 1)).reshape(channels * 8, 1)
    first, near = lax.optimization_barrier((first, near))
    far = swap(near, "patch", 1)
    first, far, table, cover, kernel, bias, repeats = lax.optimization_barrier(
        (first, far, table, cover, toeplitz(det_weight, nband), bias, repeats)
    )

    def one_repeat():
        return place(owner[None], table, first, (near, far), cover, nband, masks)

    def any_repeats():
        rest = lax.all_to_all(buf1, "patch", split_axis=0, concat_axis=0, tiled=True)
        return place(owner[None], table, first, (rest,), cover, nband, None)

    coadd, strips = lax.cond(repeats <= 1.0, one_repeat, any_repeats)
    strips = lax.all_to_all(strips, "band", split_axis=0, concat_axis=0, tiled=True)
    detection = detect(strips, kernel, bias, channels, strip_rows)
    return (coadd[None, None], detection[None])


def solution(mesh):
    placed = (
        P("patch", "band", None, None),
        P("patch", "band", None, None),
        P("patch", "band", None, None),
        P("patch", "band", None, None),
        P("band", None, None),
        P("band", None, None),
        P("band", None),
        P(),
        P(),
    )
    return jax.shard_map(
        body,
        mesh=mesh,
        in_specs=placed,
        out_specs=(P("patch", "band", None, None), P("patch", None, "band", None)),
        check_vma=False,
    )
```

```python
import jax
import jax.numpy as jnp
from jax import lax
from jax.experimental import pallas as pl
from jax.experimental.pallas import tpu as pltpu
from jax.sharding import PartitionSpec as P

PS = 512
S = 128
TAPS = 7
HALF = TAPS // 2
KS = 5
PAD = KS // 2
LANES = 128
F32 = jnp.float32
BF16 = jnp.bfloat16


def dot_nt(a, b):
    return lax.dot_general(a, b, (((1,), (1,)), ((), ())), preferred_element_type=F32)


def dot_nn(a, b):
    return lax.dot_general(a, b, (((1,), (0,)), ((), ())), preferred_element_type=F32)


def warp_tiles(here, base, offs_ref, wts_ref, taps_ref, tiles, rows, cols):
    diag = lax.broadcasted_iota(jnp.int32, (S, S), 1) - lax.broadcasted_iota(jnp.int32, (S, S), 0)

    def band(first_tap, tile):
        matrix = jnp.zeros((S, S), F32)
        for tap in range(TAPS):
            matrix = jnp.where(diag == tap - HALF, taps_ref[first_tap + tap, tile], matrix)
        return matrix.astype(BF16)

    each = range(len(here))
    psf_rows = [band(0, t) for t in here]
    psf_cols = [band(TAPS, t) for t in here]
    half_done = [dot_nt(tiles[k], psf_cols[k]).astype(BF16) for k in each]
    matched = [dot_nn(psf_rows[k], half_done[k]).astype(BF16) for k in each]
    across = [dot_nt(matched[k], cols[k]).astype(BF16) for k in each]
    product = [dot_nn(rows[k], across[k]) for k in each]
    out = []
    for k in each:
        place = base + here[k]
        warped = wts_ref[0, place] * product[k]
        warped = pltpu.roll(warped, offs_ref[1, place] & (LANES - 1), 1)
        warped = pltpu.roll(warped, offs_ref[0, place] & 7, 0)
        out.append(warped.astype(BF16))
    return out


def repeat_kernel(
    tiles, owner_ref, routes_ref, offs_ref, wts_ref, taps_ref,
    exp_ref, rows_ref, cols_ref, out_ref, held, count, found, sems,
):
    base = owner_ref[0] * tiles
    found[0] = 0

    @pl.loop(0, count.shape[0])
    def _(i):
        count[i] = 0

    @pl.loop(0, tiles)
    def _(i):
        dest = routes_ref[0, base + i]
        rank = count[dest]
        count[dest] = rank + 1
        found[0] = jnp.where(rank > 0, i, found[0])

    tile = found[0]
    copies = [
        pltpu.make_async_copy(src.at[tile, 0], held.at[i], sems.at[i])
        for i, src in enumerate((exp_ref, rows_ref, cols_ref))
    ]
    for copy in copies:
        copy.start()
    for copy in copies:
        copy.wait()
    out_ref[0] = warp_tiles(
        [tile], base, offs_ref, wts_ref, taps_ref, [held[0]], [held[1]], [held[2]]
    )[0]


def repeat(owner, routes, offs, wts, taps, exposures, warp_rows, warp_cols, npatch):
    anywhere = pl.BlockSpec(memory_space=pl.ANY)
    return pl.pallas_call(
        lambda *refs: repeat_kernel(exposures.shape[0], *refs),
        name="repeat",
        out_shape=jax.ShapeDtypeStruct((1, S, S), BF16),
        grid_spec=pltpu.PrefetchScalarGridSpec(
            num_scalar_prefetch=5,
            grid=(1,),
            in_specs=[anywhere] * 3,
            out_specs=pl.BlockSpec((1, S, S), lambda i, *_: (0, 0, 0)),
            scratch_shapes=[
                pltpu.VMEM((3, S, S), BF16),
                pltpu.SMEM((npatch,), jnp.int32),
                pltpu.SMEM((1,), jnp.int32),
                pltpu.SemaphoreType.DMA((3,)),
            ],
        ),
    )(owner, routes, offs, wts, taps, exposures, warp_rows, warp_cols)


def front_kernel(
    per_step, owner_ref, routes_ref, offs_ref, wts_ref, taps_ref,
    exp_ref, rows_ref, cols_ref, buf0_ref, buf1_ref, stage, count, sems,
):
    step = pl.program_id(0)
    steps = pl.num_programs(0)
    tiles = stage.shape[0]
    base = owner_ref[0] * tiles

    @pl.when(step == 0)
    def _():
        @pl.loop(0, count.shape[0])
        def _(i):
            count[i] = 0

    here = [step * per_step + k for k in range(per_step)]
    inputs = [[ref[k] for k in range(per_step)] for ref in (exp_ref, rows_ref, cols_ref)]
    warped = warp_tiles(here, base, offs_ref, wts_ref, taps_ref, *inputs)
    for tile, value in zip(here, warped):
        stage[tile] = value
    for tile in here:
        dest = routes_ref[0, base + tile]
        rank = count[dest]
        count[dest] = rank + 1

        @pl.when(rank == 0)
        def _():
            pltpu.make_async_copy(stage.at[tile], buf0_ref.at[dest], sems.at[tile]).start()

        @pl.when(rank > 0)
        def _():
            pltpu.make_async_copy(stage.at[tile], buf1_ref.at[dest], sems.at[tile]).start()

    @pl.when(step == steps - 1)
    def _():
        @pl.loop(0, tiles)
        def _(i):
            pltpu.make_async_copy(stage.at[i], buf0_ref.at[0], sems.at[i]).wait()


def front(owner, routes, offs, wts, taps, exposures, warp_rows, warp_cols, npatch):
    tiles = exposures.shape[0]
    per_step = 16
    spec = pl.BlockSpec((per_step, None, S, S), lambda i, *_: (i, 0, 0, 0))
    anywhere = pl.BlockSpec(memory_space=pl.ANY)
    return pl.pallas_call(
        lambda *refs: front_kernel(per_step, *refs),
        name="front",
        out_shape=(
            jax.ShapeDtypeStruct((npatch, S, S), BF16),
            jax.ShapeDtypeStruct((npatch, S, S), BF16),
        ),
        cost_estimate=pl.CostEstimate(flops=0, bytes_accessed=24 << 20, transcendentals=0),
        grid_spec=pltpu.PrefetchScalarGridSpec(
            num_scalar_prefetch=5,
            grid=(tiles // per_step,),
            in_specs=[spec, spec, spec],
            out_specs=(anywhere, anywhere),
            scratch_shapes=[
                pltpu.VMEM((tiles, S, S), BF16),
                pltpu.SMEM((npatch,), jnp.int32),
                pltpu.SemaphoreType.DMA((tiles,)),
            ],
        ),
        compiler_params=pltpu.CompilerParams(
            dimension_semantics=("arbitrary",)
        ),
    )(owner, routes, offs, wts, taps, exposures, warp_rows, warp_cols)


def spread(index, masks):
    total = 0
    for bit, mask in enumerate(masks):
        total = total | (((index >> bit) & 1) * mask)
    return total


def swap(x, axis, mask):
    size = lax.axis_size(axis)
    return lax.ppermute(x, axis, [(i, i ^ mask) for i in range(size)])


def place_kernel(per_step, nband, masks, owner_ref, table_ref, first_ref, *refs):
    second_refs, (cover_ref, coadd_ref, *strip_refs), (acc, full) = (
        refs[: -nband - 4], refs[-nband - 4 : -2], refs[-2:]
    )
    step = pl.program_id(0)
    steps = pl.num_programs(0)
    strip_rows = PS // nband
    parts = PS // LANES

    @pl.when(step == 0)
    def _():
        acc[...] = jnp.zeros_like(acc)

    lane = lax.broadcasted_iota(jnp.int32, (8, LANES), 1)
    sub = lax.broadcasted_iota(jnp.int32, (8, LANES), 0)
    for slot, src in ((0, first_ref), *((1 + i, ref) for i, ref in enumerate(second_refs))):
        for k in range(src.shape[0]):
            source = step * src.shape[0] + k
            if slot > 1:
                source = source + (slot - 1) * src.shape[0] * steps
            if slot and masks:
                source = owner_ref[0] ^ spread(source, masks)
            code = table_ref[min(slot, 1), source]

            @pl.when(code > 0)
            def _():
                corner = code - 1
                top = corner // PS
                left = corner & (PS - 1)
                base = pl.multiple_of((top // 8) * 8, 8)
                shift = top & 7
                part = left // LANES
                on = lane >= (left & (LANES - 1))
                tile = src[k].astype(F32)
                for g in range(S // 8):
                    rows = tile[8 * g : 8 * g + 8]
                    if g == 0:
                        low = jnp.where(sub < shift, rows, 0.0)
                        rows = rows - low
                        at = pl.ds(base + S, 8)
                        acc[part, at, :] += jnp.where(on, low, 0.0)
                        acc[part + 1, at, :] += jnp.where(on, 0.0, low)
                    at = pl.ds(base + 8 * g, 8)
                    acc[part, at, :] += jnp.where(on, rows, 0.0)
                    acc[part + 1, at, :] += jnp.where(on, 0.0, rows)

    @pl.when(step == steps - 1)
    def _():
        edge = full.shape[0] - PS
        full[0 : edge // 2, :] = jnp.zeros((edge // 2, PS), F32)
        full[PS + edge // 2 :, :] = jnp.zeros((edge // 2, PS), F32)
        for part in range(parts):
            at = slice(part * LANES, part * LANES + LANES)
            value = (acc[part, 0:PS, :] / jnp.maximum(cover_ref[:, at], 1.0)).astype(BF16)
            coadd_ref[:, at] = value
            full[edge // 2 : edge // 2 + PS, at] = value.astype(F32)
        height = strip_refs[0].shape[0]
        for i, ref in enumerate(strip_refs):
            start = pl.multiple_of((owner_ref[1] ^ i) * strip_rows, 8)
            rows = full[pl.ds(start, height + 8), :]
            ref[...] = rows[edge // 2 - PAD : edge // 2 - PAD + height].astype(BF16)


def place(owner, table, first, seconds, cover, nband, masks):
    per_step = 16
    steps = first.shape[0] // per_step
    strip = PS // nband + 8
    specs = [
        pl.BlockSpec((x.shape[0] // steps, S, S), lambda i, *_: (i, 0, 0)) for x in (first, *seconds)
    ]
    return pl.pallas_call(
        lambda *refs: place_kernel(per_step, nband, masks, *refs),
        name="place",
        out_shape=(
            jax.ShapeDtypeStruct((PS, PS), BF16),
            *[jax.ShapeDtypeStruct((strip, PS), BF16)] * nband,
        ),
        grid_spec=pltpu.PrefetchScalarGridSpec(
            num_scalar_prefetch=2,
            grid=(steps,),
            in_specs=[*specs, pl.BlockSpec((PS, PS), lambda i, *_: (0, 0))],
            out_specs=(
                pl.BlockSpec((PS, PS), lambda i, *_: (0, 0)),
                *[pl.BlockSpec((strip, PS), lambda i, *_: (0, 0))] * nband,
            ),
            scratch_shapes=[
                pltpu.VMEM((PS // LANES + 1, PS + 8, LANES), F32),
                pltpu.VMEM((PS + 16, PS), F32),
            ],
        ),
        compiler_params=pltpu.CompilerParams(
            dimension_semantics=("arbitrary",)
        ),
    )(owner, table, first, *seconds, cover)


def detect_kernel(nband, *refs):
    strip_refs, (weight_ref, bias_ref, out_ref, main, edge) = refs[:nband], refs[nband:]
    step = pl.program_id(0)
    groups = main.shape[0]
    channels = out_ref.shape[0]

    @pl.when(step == 0)
    def _():
        column = lax.broadcasted_iota(jnp.int32, (8, PS), 1)
        for g in range(groups):
            pieces = []
            for s in range(KS):
                for b in range(nband):
                    x = strip_refs[b][8 * g : 8 * g + 8, :].astype(F32)
                    d = s - PAD
                    if d:
                        x = pltpu.roll(x, (-d) % PS, 1)
                        x = jnp.where((column + d >= 0) & (column + d < PS), x, 0.0)
                    pieces.append(x)
            main[g] = jnp.concatenate(pieces, axis=0).astype(BF16)
            pairs = []
            for i in range(0, len(pieces), 2):
                pairs.append(pieces[i][0:4])
                pairs.append(pieces[i + 1][0:4])
            edge[g] = jnp.concatenate(pairs, axis=0).astype(BF16)

    per_step = out_ref.shape[1] // 8
    for i in range(per_step):
        g = step * per_step + i
        rhs = jnp.concatenate([main[g], edge[g + 1]], axis=0)
        res = dot_nn(weight_ref[...], rhs) + bias_ref[...]
        out_ref[:, 8 * i : 8 * i + 8, :] = res.reshape(channels, 8, PS).astype(BF16)


def detect(strips, weight, bias, channels, strip_rows):
    nband = len(strips)
    rows = strips[0].shape[0]
    groups = rows // 8
    depth = nband * KS
    step_rows = 32
    return pl.pallas_call(
        lambda *refs: detect_kernel(nband, *refs),
        name="detect",
        out_shape=jax.ShapeDtypeStruct((channels, strip_rows, PS), BF16),
        grid_spec=pltpu.PrefetchScalarGridSpec(
            num_scalar_prefetch=0,
            grid=(strip_rows // step_rows,),
            in_specs=[
                *[pl.BlockSpec(x.shape, lambda i: (0, 0)) for x in strips],
                pl.BlockSpec(weight.shape, lambda i: (0, 0)),
                pl.BlockSpec(bias.shape, lambda i: (0, 0)),
            ],
            out_specs=pl.BlockSpec((channels, step_rows, PS), lambda i: (0, i, 0)),
            scratch_shapes=[
                pltpu.VMEM((groups, depth * 8, PS), BF16),
                pltpu.VMEM((groups, depth * 4, PS), BF16),
            ],
        ),
        compiler_params=pltpu.CompilerParams(
            dimension_semantics=("arbitrary",), vmem_limit_bytes=24 << 20
        ),
    )(*strips, weight, bias)


def toeplitz(det_weight, nband, band):
    channels = det_weight.shape[0]
    taps = det_weight.reshape(channels, nband, KS, KS).transpose(0, 3, 1, 2)
    order = jnp.arange(nband) ^ band
    taps = sum(
        jnp.where((order == b)[None, None, :, None], taps[:, :, b : b + 1], 0) for b in range(nband)
    )
    row_out = jnp.arange(8)[:, None]
    out = []
    for lo, hi in ((0, 8), (8, 12)):
        row_in = jnp.arange(lo, hi)[None, :]
        total = jnp.zeros((channels, 8, KS, nband, hi - lo), det_weight.dtype)
        for r in range(KS):
            on = (row_in - row_out == r)[None, :, None, None, :]
            total = jnp.where(on, taps[:, None, :, :, r, None], total)
        out.append(total.reshape(channels * 8, KS * nband * (hi - lo)))
    return jnp.concatenate(out, axis=1)


def slot_select(targets, capacity):
    counts = jnp.cumsum(targets.astype(jnp.int32), axis=1) - 1
    slot_ids = jnp.arange(capacity, dtype=jnp.int32)
    return targets[None] & (counts[None] == slot_ids[:, None, None])


def body(exposures, psf_taps, warp_rows, warp_cols, routes, offsets, weights, det_weight, det_bias):
    npatch = lax.axis_size("patch")
    nband = lax.axis_size("band")
    tiles = exposures.shape[0]
    capacity = 2
    owner = lax.axis_index("patch").astype(jnp.int32)
    routes_row = routes.transpose(0, 2, 1).reshape(1, -1)
    offs_rows = offsets.transpose(0, 2, 1).reshape(2, -1)
    taps = psf_taps[:, 0].transpose(1, 2, 0).reshape(2 * TAPS, tiles).astype(F32)
    inputs = (owner[None], routes_row, offs_rows, weights, taps, exposures, warp_rows, warp_cols)
    near = repeat(*inputs, npatch)
    bits = npatch.bit_length() - 1
    masks = [1 << bit for bit in [*range(3, bits), 1, 2, 0] if bit < bits]
    near = [near] + [swap(near, "patch", mask) for mask in range(8, npatch, 8)]
    buf0, buf1 = front(*inputs, npatch)
    buf0, near, routes_row, offs_rows, weights, det_weight, det_bias = lax.optimization_barrier(
        (buf0, near, routes_row, offs_rows, weights, det_weight, det_bias)
    )
    near = jnp.concatenate(near, axis=0)
    near = jnp.concatenate([near] + [swap(near, "patch", m) for m in (2, 4, 6)], axis=0)
    far = swap(near, "patch", 1)
    first = lax.all_to_all(buf0, "patch", split_axis=0, concat_axis=0, tiled=True)
    dest_all = routes_row.reshape(npatch, tiles)
    same = (dest_all[:, :, None] == dest_all[:, None, :]) & (
        jnp.arange(tiles)[None, :, None] > jnp.arange(tiles)[None, None, :]
    )
    repeats = jnp.max(jnp.sum(jnp.any(same, axis=2).astype(F32), axis=1))
    for bit in range(nband.bit_length() - 1):
        repeats = jnp.maximum(repeats, swap(repeats, "band", 1 << bit))
    landed = slot_select(dest_all == owner, capacity)
    corner = (offs_rows[0] * PS + offs_rows[1] + 1).reshape(npatch, tiles)
    table = jnp.sum(jnp.where(landed, corner[None], 0), axis=-1)
    slot_weights = jnp.sum(
        jnp.where(landed, weights.reshape(npatch, tiles)[None], 0.0), axis=-1
    ).reshape(-1)
    slot_corner = jnp.maximum(table.reshape(-1) - 1, 0)
    pixels = jnp.arange(PS, dtype=jnp.int32)
    down = pixels[None, :] - (slot_corner // PS)[:, None]
    right = pixels[None, :] - (slot_corner % PS)[:, None]
    row_cover = jnp.where((down >= 0) & (down < S), slot_weights[:, None], 0.0)
    col_cover = ((right >= 0) & (right < S)).astype(F32)
    cover = jnp.einsum("ky,kx->yx", row_cover, col_cover, precision=lax.Precision.HIGHEST)
    channels = det_weight.shape[0]
    strip_rows = PS // nband
    bias = jnp.broadcast_to(det_bias[:, None, None], (channels, 8, 1)).reshape(channels * 8, 1)
    band = lax.axis_index("band").astype(jnp.int32)
    first, near, far, table, cover, kernel, bias, repeats = lax.optimization_barrier(
        (first, near, far, table, cover, toeplitz(det_weight, nband, band), bias, repeats)
    )
    where = jnp.stack([owner, band])

    def one_repeat():
        return place(where, table, first, (near, far), cover, nband, masks)

    def any_repeats():
        rest = lax.all_to_all(buf1, "patch", split_axis=0, concat_axis=0, tiled=True)
        return place(where, table, first, (rest,), cover, nband, None)

    coadd, *strips = lax.cond(repeats <= 1.0, one_repeat, any_repeats)
    strips = strips[:1] + [swap(x, "band", i) for i, x in enumerate(strips) if i]
    detection = detect(strips, kernel, bias, channels, strip_rows)
    return (coadd[None, None], detection[None])


def solution(mesh):
    placed = (
        P("patch", "band", None, None),
        P("patch", "band", None, None),
        P("patch", "band", None, None),
        P("patch", "band", None, None),
        P("band", None, None),
        P("band", None, None),
        P("band", None),
        P(),
        P(),
    )
    return jax.shard_map(
        body,
        mesh=mesh,
        in_specs=placed,
        out_specs=(P("patch", "band", None, None), P("patch", None, "band", None)),
        check_vma=False,
    )
```

```python
import jax
import jax.numpy as jnp
from jax import lax
from jax.experimental import pallas as pl
from jax.experimental.pallas import tpu as pltpu
from jax.sharding import PartitionSpec as P

PS = 512
S = 128
TAPS = 7
PLANE = 8
HALF = TAPS // 2
KS = 5
PAD = KS // 2
LANES = 128
F32 = jnp.float32
BF16 = jnp.bfloat16


def dot_nt(a, b):
    return lax.dot_general(a, b, (((1,), (1,)), ((), ())), preferred_element_type=F32)


def dot_nn(a, b):
    return lax.dot_general(a, b, (((1,), (0,)), ((), ())), preferred_element_type=F32)


def warp_tiles(here, base, offs_ref, wts_ref, taps_ref, tiles, rows, cols):
    diag = lax.broadcasted_iota(jnp.int32, (S, S), 1) - lax.broadcasted_iota(jnp.int32, (S, S), 0)

    def band(first_tap, tile):
        matrix = jnp.zeros((S, S), F32)
        for tap in range(TAPS):
            matrix = jnp.where(diag == tap - HALF, taps_ref[first_tap + tap, tile], matrix)
        return matrix.astype(BF16)

    each = range(len(here))
    psf_rows = [band(0, t) for t in here]
    psf_cols = [band(TAPS, t) for t in here]
    half_done = [dot_nt(tiles[k], psf_cols[k]).astype(BF16) for k in each]
    matched = [dot_nn(psf_rows[k], half_done[k]).astype(BF16) for k in each]
    across = [dot_nt(matched[k], cols[k]).astype(BF16) for k in each]
    product = [dot_nn(rows[k], across[k]) for k in each]
    out = []
    for k in each:
        place = base + here[k]
        warped = wts_ref[0, place] * product[k]
        warped = pltpu.roll(warped, offs_ref[1, place] & (LANES - 1), 1)
        warped = pltpu.roll(warped, offs_ref[0, place] & 7, 0)
        out.append(warped.astype(BF16))
    return out


def front_kernel(
    per_step, owner_ref, routes_ref, offs_ref, wts_ref, taps_ref,
    exp_ref, rows_ref, cols_ref, buf0_ref, buf1_ref, extra_ref, stage, count, sems,
):
    step = pl.program_id(0)
    steps = pl.num_programs(0)
    tiles = stage.shape[0]
    base = owner_ref[0] * tiles

    @pl.when(step == 0)
    def _():
        @pl.loop(0, count.shape[0])
        def _(i):
            count[i] = 0

    here = [step * per_step + k for k in range(per_step)]
    inputs = [[ref[k] for k in range(per_step)] for ref in (exp_ref, rows_ref, cols_ref)]
    warped = warp_tiles(here, base, offs_ref, wts_ref, taps_ref, *inputs)
    for tile, value in zip(here, warped):
        stage[tile] = value
    for tile in here:
        dest = routes_ref[0, base + tile]
        rank = count[dest]
        count[dest] = rank + 1

        @pl.when(rank == 0)
        def _():
            pltpu.make_async_copy(stage.at[tile], buf0_ref.at[dest], sems.at[tile]).start()

        @pl.when(rank > 0)
        def _():
            extra_ref[...] = jnp.broadcast_to(stage[tile][None], extra_ref.shape)
            pltpu.make_async_copy(stage.at[tile], buf1_ref.at[dest], sems.at[tile]).start()

    @pl.when(step == steps - 1)
    def _():
        @pl.loop(0, tiles)
        def _(i):
            pltpu.make_async_copy(stage.at[i], buf0_ref.at[0], sems.at[i]).wait()


def front(owner, routes, offs, wts, taps, exposures, warp_rows, warp_cols, npatch, copies):
    tiles = exposures.shape[0]
    per_step = 16
    spec = pl.BlockSpec((per_step, None, S, S), lambda i, *_: (i, 0, 0, 0))
    anywhere = pl.BlockSpec(memory_space=pl.ANY)
    return pl.pallas_call(
        lambda *refs: front_kernel(per_step, *refs),
        name="front",
        out_shape=(
            jax.ShapeDtypeStruct((npatch, S, S), BF16),
            jax.ShapeDtypeStruct((npatch, S, S), BF16),
            jax.ShapeDtypeStruct((copies, S, S), BF16),
        ),
        cost_estimate=pl.CostEstimate(flops=0, bytes_accessed=24 << 20, transcendentals=0),
        grid_spec=pltpu.PrefetchScalarGridSpec(
            num_scalar_prefetch=5,
            grid=(tiles // per_step,),
            in_specs=[spec, spec, spec],
            out_specs=(anywhere, anywhere, pl.BlockSpec((copies, S, S), lambda i, *_: (0, 0, 0))),
            scratch_shapes=[
                pltpu.VMEM((tiles, S, S), BF16),
                pltpu.SMEM((npatch,), jnp.int32),
                pltpu.SemaphoreType.DMA((tiles,)),
            ],
        ),
        compiler_params=pltpu.CompilerParams(
            dimension_semantics=("arbitrary",)
        ),
    )(owner, routes, offs, wts, taps, exposures, warp_rows, warp_cols)


def gathered_source(index, owner, rows):
    step = index // rows
    return (index % rows) * PLANE + (
        (owner % PLANE) ^ (((step & 1) << 1) | ((step & 2) << 1) | ((step & 4) >> 2))
    )


def swap(x, axis, mask):
    size = lax.axis_size(axis)
    return lax.ppermute(x, axis, [(i, i ^ mask) for i in range(size)])


def place_kernel(per_step, nband, gathered, owner_ref, table_ref, first_ref, *refs):
    second_refs, (cover_ref, coadd_ref, *strip_refs), (acc, full) = (
        refs[: -nband - 4], refs[-nband - 4 : -2], refs[-2:]
    )
    step = pl.program_id(0)
    steps = pl.num_programs(0)
    strip_rows = PS // nband
    parts = PS // LANES

    @pl.when(step == 0)
    def _():
        acc[...] = jnp.zeros_like(acc)

    lane = lax.broadcasted_iota(jnp.int32, (8, LANES), 1)
    sub = lax.broadcasted_iota(jnp.int32, (8, LANES), 0)
    for slot, src in ((0, first_ref), *((1 + i, ref) for i, ref in enumerate(second_refs))):
        for k in range(src.shape[0]):
            source = step * src.shape[0] + k
            if slot > 1:
                source = source + (slot - 1) * src.shape[0] * steps
            if slot and gathered:
                source = gathered_source(source, owner_ref[0], table_ref.shape[1] // PLANE)
            code = table_ref[min(slot, 1), source]

            @pl.when(code > 0)
            def _():
                corner = code - 1
                top = corner // PS
                left = corner & (PS - 1)
                base = pl.multiple_of((top // 8) * 8, 8)
                shift = top & 7
                part = left // LANES
                on = lane >= (left & (LANES - 1))
                tile = src[k].astype(F32)
                for g in range(S // 8):
                    rows = tile[8 * g : 8 * g + 8]
                    if g == 0:
                        low = jnp.where(sub < shift, rows, 0.0)
                        rows = rows - low
                        at = pl.ds(base + S, 8)
                        acc[part, at, :] += jnp.where(on, low, 0.0)
                        acc[part + 1, at, :] += jnp.where(on, 0.0, low)
                    at = pl.ds(base + 8 * g, 8)
                    acc[part, at, :] += jnp.where(on, rows, 0.0)
                    acc[part + 1, at, :] += jnp.where(on, 0.0, rows)

    @pl.when(step == steps - 1)
    def _():
        edge = full.shape[0] - PS
        full[0 : edge // 2, :] = jnp.zeros((edge // 2, PS), F32)
        full[PS + edge // 2 :, :] = jnp.zeros((edge // 2, PS), F32)
        for part in range(parts):
            at = slice(part * LANES, part * LANES + LANES)
            value = (acc[part, 0:PS, :] / jnp.maximum(cover_ref[:, at], 1.0)).astype(BF16)
            coadd_ref[:, at] = value
            full[edge // 2 : edge // 2 + PS, at] = value.astype(F32)
        height = strip_refs[0].shape[0]
        for i, ref in enumerate(strip_refs):
            start = pl.multiple_of((owner_ref[1] ^ i) * strip_rows, 8)
            rows = full[pl.ds(start, height + 8), :]
            ref[...] = rows[edge // 2 - PAD : edge // 2 - PAD + height].astype(BF16)


def place(owner, table, first, seconds, cover, nband, gathered):
    per_step = 16
    steps = first.shape[0] // per_step
    strip = PS // nband + 8
    specs = [
        pl.BlockSpec((x.shape[0] // steps, S, S), lambda i, *_: (i, 0, 0)) for x in (first, *seconds)
    ]
    return pl.pallas_call(
        lambda *refs: place_kernel(per_step, nband, gathered, *refs),
        name="place",
        out_shape=(
            jax.ShapeDtypeStruct((PS, PS), BF16),
            *[jax.ShapeDtypeStruct((strip, PS), BF16)] * nband,
        ),
        grid_spec=pltpu.PrefetchScalarGridSpec(
            num_scalar_prefetch=2,
            grid=(steps,),
            in_specs=[*specs, pl.BlockSpec((PS, PS), lambda i, *_: (0, 0))],
            out_specs=(
                pl.BlockSpec((PS, PS), lambda i, *_: (0, 0)),
                *[pl.BlockSpec((strip, PS), lambda i, *_: (0, 0))] * nband,
            ),
            scratch_shapes=[
                pltpu.VMEM((PS // LANES + 1, PS + 8, LANES), F32),
                pltpu.VMEM((PS + 16, PS), F32),
            ],
        ),
        compiler_params=pltpu.CompilerParams(
            dimension_semantics=("arbitrary",)
        ),
    )(owner, table, first, *seconds, cover)


def detect_kernel(nband, *refs):
    strip_refs, (weight_ref, bias_ref, out_ref, main, edge) = refs[:nband], refs[nband:]
    step = pl.program_id(0)
    groups = main.shape[0]
    channels = out_ref.shape[0]

    @pl.when(step == 0)
    def _():
        column = lax.broadcasted_iota(jnp.int32, (8, PS), 1)
        for g in range(groups):
            pieces = []
            for s in range(KS):
                for b in range(nband):
                    x = strip_refs[b][8 * g : 8 * g + 8, :].astype(F32)
                    d = s - PAD
                    if d:
                        x = pltpu.roll(x, (-d) % PS, 1)
                        x = jnp.where((column + d >= 0) & (column + d < PS), x, 0.0)
                    pieces.append(x)
            main[g] = jnp.concatenate(pieces, axis=0).astype(BF16)
            pairs = []
            for i in range(0, len(pieces), 2):
                pairs.append(pieces[i][0:4])
                pairs.append(pieces[i + 1][0:4])
            edge[g] = jnp.concatenate(pairs, axis=0).astype(BF16)

    per_step = out_ref.shape[1] // 8
    for i in range(per_step):
        g = step * per_step + i
        rhs = jnp.concatenate([main[g], edge[g + 1]], axis=0)
        res = dot_nn(weight_ref[...], rhs) + bias_ref[...]
        out_ref[:, 8 * i : 8 * i + 8, :] = res.reshape(channels, 8, PS).astype(BF16)


def detect(strips, weight, bias, channels, strip_rows):
    nband = len(strips)
    rows = strips[0].shape[0]
    groups = rows // 8
    depth = nband * KS
    step_rows = 32
    return pl.pallas_call(
        lambda *refs: detect_kernel(nband, *refs),
        name="detect",
        out_shape=jax.ShapeDtypeStruct((channels, strip_rows, PS), BF16),
        grid_spec=pltpu.PrefetchScalarGridSpec(
            num_scalar_prefetch=0,
            grid=(strip_rows // step_rows,),
            in_specs=[
                *[pl.BlockSpec(x.shape, lambda i: (0, 0)) for x in strips],
                pl.BlockSpec(weight.shape, lambda i: (0, 0)),
                pl.BlockSpec(bias.shape, lambda i: (0, 0)),
            ],
            out_specs=pl.BlockSpec((channels, step_rows, PS), lambda i: (0, i, 0)),
            scratch_shapes=[
                pltpu.VMEM((groups, depth * 8, PS), BF16),
                pltpu.VMEM((groups, depth * 4, PS), BF16),
            ],
        ),
        compiler_params=pltpu.CompilerParams(
            dimension_semantics=("arbitrary",), vmem_limit_bytes=24 << 20
        ),
    )(*strips, weight, bias)


def toeplitz(det_weight, nband, band):
    channels = det_weight.shape[0]
    taps = det_weight.reshape(channels, nband, KS, KS).transpose(0, 3, 1, 2)
    order = jnp.arange(nband) ^ band
    taps = sum(
        jnp.where((order == b)[None, None, :, None], taps[:, :, b : b + 1], 0) for b in range(nband)
    )
    row_out = jnp.arange(8)[:, None]
    out = []
    for lo, hi in ((0, 8), (8, 12)):
        row_in = jnp.arange(lo, hi)[None, :]
        total = jnp.zeros((channels, 8, KS, nband, hi - lo), det_weight.dtype)
        for r in range(KS):
            on = (row_in - row_out == r)[None, :, None, None, :]
            total = jnp.where(on, taps[:, None, :, :, r, None], total)
        out.append(total.reshape(channels * 8, KS * nband * (hi - lo)))
    return jnp.concatenate(out, axis=1)


def slot_select(targets, capacity):
    counts = jnp.cumsum(targets.astype(jnp.int32), axis=1) - 1
    slot_ids = jnp.arange(capacity, dtype=jnp.int32)
    return targets[None] & (counts[None] == slot_ids[:, None, None])


def body(exposures, psf_taps, warp_rows, warp_cols, routes, offsets, weights, det_weight, det_bias):
    npatch = lax.axis_size("patch")
    nband = lax.axis_size("band")
    tiles = exposures.shape[0]
    capacity = 2
    owner = lax.axis_index("patch").astype(jnp.int32)
    routes_row = routes.transpose(0, 2, 1).reshape(1, -1)
    offs_rows = offsets.transpose(0, 2, 1).reshape(2, -1)
    taps = psf_taps[:, 0].transpose(1, 2, 0).reshape(2 * TAPS, tiles).astype(F32)
    inputs = (owner[None], routes_row, offs_rows, weights, taps, exposures, warp_rows, warp_cols)
    buf0, buf1, extra = front(*inputs, npatch, npatch // PLANE)
    lines = [list(range(i, npatch, PLANE)) for i in range(PLANE)]
    near = lax.all_to_all(
        extra, "patch", split_axis=0, concat_axis=0, axis_index_groups=lines, tiled=True
    )
    buf0, near, routes_row, offs_rows, weights, det_weight, det_bias = lax.optimization_barrier(
        (buf0, near, routes_row, offs_rows, weights, det_weight, det_bias)
    )
    near = jnp.concatenate([near] + [swap(near, "patch", m) for m in (2, 4, 6)], axis=0)
    far = swap(near, "patch", 1)
    first = lax.all_to_all(buf0, "patch", split_axis=0, concat_axis=0, tiled=True)
    dest_all = routes_row.reshape(npatch, tiles)
    same = (dest_all[:, :, None] == dest_all[:, None, :]) & (
        jnp.arange(tiles)[None, :, None] > jnp.arange(tiles)[None, None, :]
    )
    repeats = jnp.max(jnp.sum(jnp.any(same, axis=2).astype(F32), axis=1))
    for bit in range(nband.bit_length() - 1):
        repeats = jnp.maximum(repeats, swap(repeats, "band", 1 << bit))
    landed = slot_select(dest_all == owner, capacity)
    corner = (offs_rows[0] * PS + offs_rows[1] + 1).reshape(npatch, tiles)
    table = jnp.sum(jnp.where(landed, corner[None], 0), axis=-1)
    slot_weights = jnp.sum(
        jnp.where(landed, weights.reshape(npatch, tiles)[None], 0.0), axis=-1
    ).reshape(-1)
    slot_corner = jnp.maximum(table.reshape(-1) - 1, 0)
    pixels = jnp.arange(PS, dtype=jnp.int32)
    down = pixels[None, :] - (slot_corner // PS)[:, None]
    right = pixels[None, :] - (slot_corner % PS)[:, None]
    row_cover = jnp.where((down >= 0) & (down < S), slot_weights[:, None], 0.0)
    col_cover = ((right >= 0) & (right < S)).astype(F32)
    cover = jnp.einsum("ky,kx->yx", row_cover, col_cover, precision=lax.Precision.HIGHEST)
    channels = det_weight.shape[0]
    strip_rows = PS // nband
    bias = jnp.broadcast_to(det_bias[:, None, None], (channels, 8, 1)).reshape(channels * 8, 1)
    band = lax.axis_index("band").astype(jnp.int32)
    first, near, far, table, cover, kernel, bias, repeats = lax.optimization_barrier(
        (first, near, far, table, cover, toeplitz(det_weight, nband, band), bias, repeats)
    )
    where = jnp.stack([owner, band])

    def one_repeat():
        return place(where, table, first, (near, far), cover, nband, True)

    def any_repeats():
        rest = lax.all_to_all(buf1, "patch", split_axis=0, concat_axis=0, tiled=True)
        return place(where, table, first, (rest,), cover, nband, False)

    coadd, *strips = lax.cond(repeats <= 1.0, one_repeat, any_repeats)
    strips = strips[:1] + [swap(x, "band", i) for i, x in enumerate(strips) if i]
    detection = detect(strips, kernel, bias, channels, strip_rows)
    return (coadd[None, None], detection[None])


def solution(mesh):
    placed = (
        P("patch", "band", None, None),
        P("patch", "band", None, None),
        P("patch", "band", None, None),
        P("patch", "band", None, None),
        P("band", None, None),
        P("band", None, None),
        P("band", None),
        P(),
        P(),
    )
    return jax.shard_map(
        body,
        mesh=mesh,
        in_specs=placed,
        out_specs=(P("patch", "band", None, None), P("patch", None, "band", None)),
        check_vma=False,
    )
```

```python
import jax
import jax.numpy as jnp
from jax import lax
from jax.experimental import pallas as pl
from jax.experimental.pallas import tpu as pltpu
from jax.sharding import PartitionSpec as P

PS = 512
S = 128
TAPS = 7
PLANE = 8
HALF = TAPS // 2
KS = 5
PAD = KS // 2
LANES = 128
F32 = jnp.float32
BF16 = jnp.bfloat16


def dot_nt(a, b):
    return lax.dot_general(a, b, (((1,), (1,)), ((), ())), preferred_element_type=F32)


def dot_nn(a, b):
    return lax.dot_general(a, b, (((1,), (0,)), ((), ())), preferred_element_type=F32)


def warp_tiles(here, base, offs_ref, wts_ref, taps_ref, tiles, rows, cols):
    diag = lax.broadcasted_iota(jnp.int32, (S, S), 1) - lax.broadcasted_iota(jnp.int32, (S, S), 0)

    def band(first_tap, tile):
        matrix = jnp.zeros((S, S), F32)
        for tap in range(TAPS):
            matrix = jnp.where(diag == tap - HALF, taps_ref[first_tap + tap, tile], matrix)
        return matrix.astype(BF16)

    each = range(len(here))
    psf_rows = [band(0, t) for t in here]
    psf_cols = [band(TAPS, t) for t in here]
    half_done = [dot_nt(tiles[k], psf_cols[k]).astype(BF16) for k in each]
    matched = [dot_nn(psf_rows[k], half_done[k]).astype(BF16) for k in each]
    across = [dot_nt(matched[k], cols[k]).astype(BF16) for k in each]
    product = [dot_nn(rows[k], across[k]) for k in each]
    out = []
    for k in each:
        place = base + here[k]
        warped = wts_ref[0, place] * product[k]
        warped = pltpu.roll(warped, offs_ref[1, place] & (LANES - 1), 1)
        warped = pltpu.roll(warped, offs_ref[0, place] & 7, 0)
        out.append(warped.astype(BF16))
    return out


def repeat_kernel(
    tiles, owner_ref, routes_ref, offs_ref, wts_ref, taps_ref,
    exp_ref, rows_ref, cols_ref, out_ref, held, count, found, sems,
):
    base = owner_ref[0] * tiles
    found[0] = 0

    @pl.loop(0, count.shape[0])
    def _(i):
        count[i] = 0

    @pl.loop(0, tiles)
    def _(i):
        dest = routes_ref[0, base + i]
        rank = count[dest]
        count[dest] = rank + 1
        found[0] = jnp.where(rank > 0, i, found[0])

    tile = found[0]
    copies = [
        pltpu.make_async_copy(src.at[tile, 0], held.at[i], sems.at[i])
        for i, src in enumerate((exp_ref, rows_ref, cols_ref))
    ]
    for copy in copies:
        copy.start()
    for copy in copies:
        copy.wait()
    warped = warp_tiles(
        [tile], base, offs_ref, wts_ref, taps_ref, [held[0]], [held[1]], [held[2]]
    )
    out_ref[...] = jnp.broadcast_to(warped[0][None], out_ref.shape)


def repeat(owner, routes, offs, wts, taps, exposures, warp_rows, warp_cols, npatch, copies):
    anywhere = pl.BlockSpec(memory_space=pl.ANY)
    return pl.pallas_call(
        lambda *refs: repeat_kernel(exposures.shape[0], *refs),
        name="repeat",
        out_shape=jax.ShapeDtypeStruct((copies, S, S), BF16),
        grid_spec=pltpu.PrefetchScalarGridSpec(
            num_scalar_prefetch=5,
            grid=(1,),
            in_specs=[anywhere] * 3,
            out_specs=pl.BlockSpec((copies, S, S), lambda i, *_: (0, 0, 0)),
            scratch_shapes=[
                pltpu.VMEM((3, S, S), BF16),
                pltpu.SMEM((npatch,), jnp.int32),
                pltpu.SMEM((1,), jnp.int32),
                pltpu.SemaphoreType.DMA((3,)),
            ],
        ),
    )(owner, routes, offs, wts, taps, exposures, warp_rows, warp_cols)


def front_kernel(
    per_step, owner_ref, routes_ref, offs_ref, wts_ref, taps_ref,
    exp_ref, rows_ref, cols_ref, buf0_ref, buf1_ref, stage, count, sems,
):
    step = pl.program_id(0)
    steps = pl.num_programs(0)
    tiles = stage.shape[0]
    base = owner_ref[0] * tiles

    @pl.when(step == 0)
    def _():
        @pl.loop(0, count.shape[0])
        def _(i):
            count[i] = 0

    here = [step * per_step + k for k in range(per_step)]
    inputs = [[ref[k] for k in range(per_step)] for ref in (exp_ref, rows_ref, cols_ref)]
    warped = warp_tiles(here, base, offs_ref, wts_ref, taps_ref, *inputs)
    for tile, value in zip(here, warped):
        stage[tile] = value
    for tile in here:
        dest = routes_ref[0, base + tile]
        rank = count[dest]
        count[dest] = rank + 1

        @pl.when(rank == 0)
        def _():
            pltpu.make_async_copy(stage.at[tile], buf0_ref.at[dest], sems.at[tile]).start()

        @pl.when(rank > 0)
        def _():
            pltpu.make_async_copy(stage.at[tile], buf1_ref.at[dest], sems.at[tile]).start()

    @pl.when(step == steps - 1)
    def _():
        @pl.loop(0, tiles)
        def _(i):
            pltpu.make_async_copy(stage.at[i], buf0_ref.at[0], sems.at[i]).wait()


def front(owner, routes, offs, wts, taps, exposures, warp_rows, warp_cols, npatch):
    tiles = exposures.shape[0]
    per_step = 16
    spec = pl.BlockSpec((per_step, None, S, S), lambda i, *_: (i, 0, 0, 0))
    anywhere = pl.BlockSpec(memory_space=pl.ANY)
    return pl.pallas_call(
        lambda *refs: front_kernel(per_step, *refs),
        name="front",
        out_shape=(
            jax.ShapeDtypeStruct((npatch, S, S), BF16),
            jax.ShapeDtypeStruct((npatch, S, S), BF16),
        ),
        cost_estimate=pl.CostEstimate(flops=0, bytes_accessed=24 << 20, transcendentals=0),
        grid_spec=pltpu.PrefetchScalarGridSpec(
            num_scalar_prefetch=5,
            grid=(tiles // per_step,),
            in_specs=[spec, spec, spec],
            out_specs=(anywhere, anywhere),
            scratch_shapes=[
                pltpu.VMEM((tiles, S, S), BF16),
                pltpu.SMEM((npatch,), jnp.int32),
                pltpu.SemaphoreType.DMA((tiles,)),
            ],
        ),
        compiler_params=pltpu.CompilerParams(
            dimension_semantics=("arbitrary",)
        ),
    )(owner, routes, offs, wts, taps, exposures, warp_rows, warp_cols)


def gathered_source(index, owner, rows):
    step = index // rows
    return (index % rows) * PLANE + (
        (owner % PLANE) ^ (((step & 1) << 1) | ((step & 2) << 1) | ((step & 4) >> 2))
    )


def swap(x, axis, mask):
    size = lax.axis_size(axis)
    return lax.ppermute(x, axis, [(i, i ^ mask) for i in range(size)])


def place_kernel(per_step, nband, gathered, owner_ref, table_ref, first_ref, *refs):
    second_refs, (cover_ref, coadd_ref, *strip_refs), (acc, full) = (
        refs[: -nband - 4], refs[-nband - 4 : -2], refs[-2:]
    )
    step = pl.program_id(0)
    steps = pl.num_programs(0)
    strip_rows = PS // nband
    parts = PS // LANES

    @pl.when(step == 0)
    def _():
        acc[...] = jnp.zeros_like(acc)

    lane = lax.broadcasted_iota(jnp.int32, (8, LANES), 1)
    sub = lax.broadcasted_iota(jnp.int32, (8, LANES), 0)
    for slot, src in ((0, first_ref), *((1 + i, ref) for i, ref in enumerate(second_refs))):
        for k in range(src.shape[0]):
            source = step * src.shape[0] + k
            if slot > 1:
                source = source + (slot - 1) * src.shape[0] * steps
            if slot and gathered:
                source = gathered_source(source, owner_ref[0], table_ref.shape[1] // PLANE)
            code = table_ref[min(slot, 1), source]

            @pl.when(code > 0)
            def _():
                corner = code - 1
                top = corner // PS
                left = corner & (PS - 1)
                base = pl.multiple_of((top // 8) * 8, 8)
                shift = top & 7
                part = left // LANES
                on = lane >= (left & (LANES - 1))
                tile = src[k].astype(F32)
                for g in range(S // 8):
                    rows = tile[8 * g : 8 * g + 8]
                    if g == 0:
                        low = jnp.where(sub < shift, rows, 0.0)
                        rows = rows - low
                        at = pl.ds(base + S, 8)
                        acc[part, at, :] += jnp.where(on, low, 0.0)
                        acc[part + 1, at, :] += jnp.where(on, 0.0, low)
                    at = pl.ds(base + 8 * g, 8)
                    acc[part, at, :] += jnp.where(on, rows, 0.0)
                    acc[part + 1, at, :] += jnp.where(on, 0.0, rows)

    @pl.when(step == steps - 1)
    def _():
        edge = full.shape[0] - PS
        full[0 : edge // 2, :] = jnp.zeros((edge // 2, PS), F32)
        full[PS + edge // 2 :, :] = jnp.zeros((edge // 2, PS), F32)
        for part in range(parts):
            at = slice(part * LANES, part * LANES + LANES)
            value = (acc[part, 0:PS, :] / jnp.maximum(cover_ref[:, at], 1.0)).astype(BF16)
            coadd_ref[:, at] = value
            full[edge // 2 : edge // 2 + PS, at] = value.astype(F32)
        height = strip_refs[0].shape[0]
        for i, ref in enumerate(strip_refs):
            start = pl.multiple_of((owner_ref[1] ^ i) * strip_rows, 8)
            rows = full[pl.ds(start, height + 8), :]
            ref[...] = rows[edge // 2 - PAD : edge // 2 - PAD + height].astype(BF16)


def place(owner, table, first, seconds, cover, nband, gathered):
    per_step = 16
    steps = first.shape[0] // per_step
    strip = PS // nband + 8
    specs = [
        pl.BlockSpec((x.shape[0] // steps, S, S), lambda i, *_: (i, 0, 0)) for x in (first, *seconds)
    ]
    return pl.pallas_call(
        lambda *refs: place_kernel(per_step, nband, gathered, *refs),
        name="place",
        out_shape=(
            jax.ShapeDtypeStruct((PS, PS), BF16),
            *[jax.ShapeDtypeStruct((strip, PS), BF16)] * nband,
        ),
        grid_spec=pltpu.PrefetchScalarGridSpec(
            num_scalar_prefetch=2,
            grid=(steps,),
            in_specs=[*specs, pl.BlockSpec((PS, PS), lambda i, *_: (0, 0))],
            out_specs=(
                pl.BlockSpec((PS, PS), lambda i, *_: (0, 0)),
                *[pl.BlockSpec((strip, PS), lambda i, *_: (0, 0))] * nband,
            ),
            scratch_shapes=[
                pltpu.VMEM((PS // LANES + 1, PS + 8, LANES), F32),
                pltpu.VMEM((PS + 16, PS), F32),
            ],
        ),
        compiler_params=pltpu.CompilerParams(
            dimension_semantics=("arbitrary",)
        ),
    )(owner, table, first, *seconds, cover)


def detect_kernel(nband, *refs):
    strip_refs, (weight_ref, bias_ref, out_ref, main, edge) = refs[:nband], refs[nband:]
    step = pl.program_id(0)
    groups = main.shape[0]
    channels = out_ref.shape[0]

    @pl.when(step == 0)
    def _():
        column = lax.broadcasted_iota(jnp.int32, (8, PS), 1)
        for g in range(groups):
            pieces = []
            for s in range(KS):
                for b in range(nband):
                    x = strip_refs[b][8 * g : 8 * g + 8, :].astype(F32)
                    d = s - PAD
                    if d:
                        x = pltpu.roll(x, (-d) % PS, 1)
                        x = jnp.where((column + d >= 0) & (column + d < PS), x, 0.0)
                    pieces.append(x)
            main[g] = jnp.concatenate(pieces, axis=0).astype(BF16)
            pairs = []
            for i in range(0, len(pieces), 2):
                pairs.append(pieces[i][0:4])
                pairs.append(pieces[i + 1][0:4])
            edge[g] = jnp.concatenate(pairs, axis=0).astype(BF16)

    per_step = out_ref.shape[1] // 8
    for i in range(per_step):
        g = step * per_step + i
        rhs = jnp.concatenate([main[g], edge[g + 1]], axis=0)
        res = dot_nn(weight_ref[...], rhs) + bias_ref[...]
        out_ref[:, 8 * i : 8 * i + 8, :] = res.reshape(channels, 8, PS).astype(BF16)


def detect(strips, weight, bias, channels, strip_rows):
    nband = len(strips)
    rows = strips[0].shape[0]
    groups = rows // 8
    depth = nband * KS
    step_rows = 32
    return pl.pallas_call(
        lambda *refs: detect_kernel(nband, *refs),
        name="detect",
        out_shape=jax.ShapeDtypeStruct((channels, strip_rows, PS), BF16),
        grid_spec=pltpu.PrefetchScalarGridSpec(
            num_scalar_prefetch=0,
            grid=(strip_rows // step_rows,),
            in_specs=[
                *[pl.BlockSpec(x.shape, lambda i: (0, 0)) for x in strips],
                pl.BlockSpec(weight.shape, lambda i: (0, 0)),
                pl.BlockSpec(bias.shape, lambda i: (0, 0)),
            ],
            out_specs=pl.BlockSpec((channels, step_rows, PS), lambda i: (0, i, 0)),
            scratch_shapes=[
                pltpu.VMEM((groups, depth * 8, PS), BF16),
                pltpu.VMEM((groups, depth * 4, PS), BF16),
            ],
        ),
        compiler_params=pltpu.CompilerParams(
            dimension_semantics=("arbitrary",), vmem_limit_bytes=24 << 20
        ),
    )(*strips, weight, bias)


def toeplitz(det_weight, nband, band):
    channels, inputs = det_weight.shape
    combos = KS * nband
    column = jnp.arange(combos * 12, dtype=jnp.int32)
    tail = column >= combos * 8
    combo = jnp.where(tail, (column - combos * 8) >> 2, column >> 3)
    row_in = jnp.where(tail, 8 + ((column - combos * 8) & 3), column & 7)
    shift, slot = combo // nband, combo % nband
    source = (slot ^ band) * (KS * KS) + shift
    rows = jnp.arange(KS, dtype=jnp.int32)[:, None] * KS + source[None, :]
    pick = (jnp.arange(inputs, dtype=jnp.int32)[:, None, None] == rows[None]).astype(BF16)
    taps = lax.dot_general(
        det_weight, pick, (((1,), (0,)), ((), ())), preferred_element_type=F32
    )
    offset = row_in[None, :] - jnp.arange(8, dtype=jnp.int32)[:, None]
    total = jnp.zeros((channels, 8, combos * 12), F32)
    for r in range(KS):
        total = jnp.where((offset == r)[None], taps[:, None, r], total)
    return total.astype(BF16).reshape(channels * 8, combos * 12)


def slot_select(targets, capacity):
    counts = jnp.cumsum(targets.astype(jnp.int32), axis=1) - 1
    slot_ids = jnp.arange(capacity, dtype=jnp.int32)
    return targets[None] & (counts[None] == slot_ids[:, None, None])


def body(exposures, psf_taps, warp_rows, warp_cols, routes, offsets, weights, det_weight, det_bias):
    npatch = lax.axis_size("patch")
    nband = lax.axis_size("band")
    tiles = exposures.shape[0]
    capacity = 2
    owner = lax.axis_index("patch").astype(jnp.int32)
    routes_row = routes.transpose(0, 2, 1).reshape(1, -1)
    offs_rows = offsets.transpose(0, 2, 1).reshape(2, -1)
    taps = psf_taps[:, 0].transpose(1, 2, 0).reshape(2 * TAPS, tiles).astype(F32)
    inputs = (owner[None], routes_row, offs_rows, weights, taps, exposures, warp_rows, warp_cols)
    extra = repeat(*inputs, npatch, npatch // PLANE)
    lines = [list(range(i, npatch, PLANE)) for i in range(PLANE)]
    near = lax.all_to_all(
        extra, "patch", split_axis=0, concat_axis=0, axis_index_groups=lines, tiled=True
    )
    buf0, buf1 = front(*inputs, npatch)
    buf0, near, routes_row, offs_rows, weights, det_weight, det_bias = lax.optimization_barrier(
        (buf0, near, routes_row, offs_rows, weights, det_weight, det_bias)
    )
    near = [near] + [swap(near, "patch", m) for m in (2, 4, 6)]
    far = [swap(x, "patch", 1) for x in near]
    first = lax.all_to_all(buf0, "patch", split_axis=0, concat_axis=0, tiled=True)
    dest_all = routes_row.reshape(npatch, tiles)
    same = (dest_all[:, :, None] == dest_all[:, None, :]) & (
        jnp.arange(tiles)[None, :, None] > jnp.arange(tiles)[None, None, :]
    )
    repeats = jnp.max(jnp.sum(jnp.any(same, axis=2).astype(F32), axis=1))
    for bit in range(nband.bit_length() - 1):
        repeats = jnp.maximum(repeats, swap(repeats, "band", 1 << bit))
    landed = slot_select(dest_all == owner, capacity)
    corner = (offs_rows[0] * PS + offs_rows[1] + 1).reshape(npatch, tiles)
    table = jnp.sum(jnp.where(landed, corner[None], 0), axis=-1)
    slot_weights = jnp.sum(
        jnp.where(landed, weights.reshape(npatch, tiles)[None], 0.0), axis=-1
    ).reshape(-1)
    slot_corner = jnp.maximum(table.reshape(-1) - 1, 0)
    pixels = jnp.arange(PS, dtype=jnp.int32)
    down = pixels[None, :] - (slot_corner >> (PS.bit_length() - 1))[:, None]
    right = pixels[None, :] - (slot_corner & (PS - 1))[:, None]
    row_cover = jnp.where((down >= 0) & (down < S), slot_weights[:, None], 0.0)
    col_cover = ((right >= 0) & (right < S)).astype(F32)
    cover = jnp.einsum("ky,kx->yx", row_cover, col_cover, precision=lax.Precision.HIGHEST)
    channels = det_weight.shape[0]
    strip_rows = PS // nband
    bias = jnp.broadcast_to(det_bias[:, None, None], (channels, 8, 1)).reshape(channels * 8, 1)
    band = lax.axis_index("band").astype(jnp.int32)
    first, near, far, table, cover, kernel, bias, repeats = lax.optimization_barrier(
        (first, near, far, table, cover, toeplitz(det_weight, nband, band), bias, repeats)
    )
    where = jnp.stack([owner, band])

    def one_repeat():
        return place(where, table, first, (*near, *far), cover, nband, True)

    def any_repeats():
        rest = lax.all_to_all(buf1, "patch", split_axis=0, concat_axis=0, tiled=True)
        return place(where, table, first, (rest,), cover, nband, False)

    coadd, *strips = lax.cond(repeats <= 1.0, one_repeat, any_repeats)
    strips = strips[:1] + [swap(x, "band", i) for i, x in enumerate(strips) if i]
    detection = detect(strips, kernel, bias, channels, strip_rows)
    return (coadd[None, None], detection[None])


def solution(mesh):
    placed = (
        P("patch", "band", None, None),
        P("patch", "band", None, None),
        P("patch", "band", None, None),
        P("patch", "band", None, None),
        P("band", None, None),
        P("band", None, None),
        P("band", None),
        P(),
        P(),
    )
    return jax.shard_map(
        body,
        mesh=mesh,
        in_specs=placed,
        out_specs=(P("patch", "band", None, None), P("patch", None, "band", None)),
        check_vma=False,
    )
```

```python
import jax
import jax.numpy as jnp
from jax import lax
from jax.experimental import pallas as pl
from jax.experimental.pallas import tpu as pltpu
from jax.sharding import PartitionSpec as P

PS = 512
S = 128
TAPS = 7
PLANE = 8
HALF = TAPS // 2
KS = 5
PAD = KS // 2
LANES = 128
F32 = jnp.float32
BF16 = jnp.bfloat16


def dot_nt(a, b):
    return lax.dot_general(a, b, (((1,), (1,)), ((), ())), preferred_element_type=F32)


def dot_nn(a, b):
    return lax.dot_general(a, b, (((1,), (0,)), ((), ())), preferred_element_type=F32)


def warp_tiles(here, base, offs_ref, wts_ref, taps_ref, tiles, rows, cols):
    diag = lax.broadcasted_iota(jnp.int32, (S, S), 1) - lax.broadcasted_iota(jnp.int32, (S, S), 0)

    def band(axis, tile):
        matrix = jnp.zeros((S, S), F32)
        for tap in range(TAPS):
            matrix = jnp.where(diag == tap - HALF, taps_ref[tap, axis, tile], matrix)
        return matrix.astype(BF16)

    each = range(len(here))
    psf_rows = [band(0, t) for t in here]
    psf_cols = [band(1, t) for t in here]
    half_done = [dot_nt(tiles[k], psf_cols[k]).astype(BF16) for k in each]
    matched = [dot_nn(psf_rows[k], half_done[k]).astype(BF16) for k in each]
    across = [dot_nt(matched[k], cols[k]).astype(BF16) for k in each]
    product = [dot_nn(rows[k], across[k]) for k in each]
    out = []
    for k in each:
        place = base + here[k]
        warped = wts_ref[0, place] * product[k]
        warped = pltpu.roll(warped, offs_ref[1, place] & (LANES - 1), 1)
        warped = pltpu.roll(warped, offs_ref[0, place] & 7, 0)
        out.append(warped.astype(BF16))
    return out


def repeat_kernel(
    tiles, owner_ref, routes_ref, offs_ref, wts_ref, taps_ref,
    exp_ref, rows_ref, cols_ref, out_ref, held, count, found, sems,
):
    base = owner_ref[0] * tiles
    found[0] = 0

    @pl.loop(0, count.shape[0], unroll=8)
    def _(i):
        count[i] = 0

    @pl.loop(0, tiles, unroll=4)
    def _(i):
        dest = routes_ref[0, base + i]
        rank = count[dest]
        count[dest] = rank + 1
        found[0] = jnp.where(rank > 0, i, found[0])

    tile = found[0]
    copies = [
        pltpu.make_async_copy(src.at[tile, 0], held.at[i], sems.at[i])
        for i, src in enumerate((exp_ref, rows_ref, cols_ref))
    ]
    for copy in copies:
        copy.start()
    for copy in copies:
        copy.wait()
    warped = warp_tiles(
        [tile], base, offs_ref, wts_ref, taps_ref, [held[0]], [held[1]], [held[2]]
    )
    out_ref[...] = jnp.broadcast_to(warped[0][None], out_ref.shape)


def repeat(owner, routes, offs, wts, taps, exposures, warp_rows, warp_cols, npatch, copies):
    anywhere = pl.BlockSpec(memory_space=pl.ANY)
    return pl.pallas_call(
        lambda *refs: repeat_kernel(exposures.shape[0], *refs),
        name="repeat",
        out_shape=jax.ShapeDtypeStruct((copies, S, S), BF16),
        grid_spec=pltpu.PrefetchScalarGridSpec(
            num_scalar_prefetch=5,
            grid=(1,),
            in_specs=[anywhere] * 3,
            out_specs=pl.BlockSpec((copies, S, S), lambda i, *_: (0, 0, 0)),
            scratch_shapes=[
                pltpu.VMEM((3, S, S), BF16),
                pltpu.SMEM((npatch,), jnp.int32),
                pltpu.SMEM((1,), jnp.int32),
                pltpu.SemaphoreType.DMA((3,)),
            ],
        ),
    )(owner, routes, offs, wts, taps, exposures, warp_rows, warp_cols)


def front_kernel(
    chunk, owner_ref, routes_ref, offs_ref, wts_ref, taps_ref,
    exp_ref, rows_ref, cols_ref, buf0_ref, buf1_ref, held, stage, count, load_sems, sems,
):
    tiles = stage.shape[0]
    base = owner_ref[0] * tiles
    loads = [
        [
            pltpu.make_async_copy(
                src.at[pl.ds(start, chunk), 0], held.at[i, pl.ds(start, chunk)], load_sems.at[i, n]
            )
            for i, src in enumerate((exp_ref, rows_ref, cols_ref))
        ]
        for n, start in enumerate(range(0, tiles, chunk))
    ]
    for copies in loads:
        for copy in copies:
            copy.start()

    @pl.loop(0, count.shape[0], unroll=8)
    def _(i):
        count[i] = 0

    for n, copies in enumerate(loads):
        for copy in copies:
            copy.wait()
        here = [n * chunk + k for k in range(chunk)]
        inputs = [[held[i, tile] for tile in here] for i in range(3)]
        warped = warp_tiles(here, base, offs_ref, wts_ref, taps_ref, *inputs)
        for tile, value in zip(here, warped):
            stage[tile] = value
        for tile in here:
            dest = routes_ref[0, base + tile]
            rank = count[dest]
            count[dest] = rank + 1

            @pl.when(rank == 0)
            def _():
                pltpu.make_async_copy(stage.at[tile], buf0_ref.at[dest], sems.at[tile]).start()

            @pl.when(rank > 0)
            def _():
                pltpu.make_async_copy(stage.at[tile], buf1_ref.at[dest], sems.at[tile]).start()

    @pl.loop(0, tiles, unroll=8)
    def _(i):
        pltpu.make_async_copy(stage.at[i], buf0_ref.at[0], sems.at[i]).wait()


def front(owner, routes, offs, wts, taps, exposures, warp_rows, warp_cols, npatch):
    tiles = exposures.shape[0]
    chunk = 16
    anywhere = pl.BlockSpec(memory_space=pl.ANY)
    scalars = pl.BlockSpec(memory_space=pltpu.SMEM)
    return pl.pallas_call(
        lambda *refs: front_kernel(chunk, *refs),
        name="front",
        out_shape=(
            jax.ShapeDtypeStruct((npatch, S, S), BF16),
            jax.ShapeDtypeStruct((npatch, S, S), BF16),
        ),
        cost_estimate=pl.CostEstimate(flops=0, bytes_accessed=24 << 20, transcendentals=0),
        in_specs=[scalars] * 5 + [anywhere] * 3,
        out_specs=(anywhere, anywhere),
        scratch_shapes=[
            pltpu.VMEM((3, tiles, S, S), BF16),
            pltpu.VMEM((tiles, S, S), BF16),
            pltpu.SMEM((npatch,), jnp.int32),
            pltpu.SemaphoreType.DMA((3, tiles // chunk)),
            pltpu.SemaphoreType.DMA((tiles,)),
        ],
    )(owner, routes, offs, wts, taps, exposures, warp_rows, warp_cols)


def gathered_source(index, owner, rows):
    step = index // rows
    return (index % rows) * PLANE + (
        (owner % PLANE) ^ (((step & 1) << 1) | ((step & 2) << 1) | ((step & 4) >> 2))
    )


def swap(x, axis, mask):
    size = lax.axis_size(axis)
    return lax.ppermute(x, axis, [(i, i ^ mask) for i in range(size)])


def place_kernel(nband, gathered, owner_ref, table_ref, first_ref, *refs):
    second_refs, (cover_ref, coadd_ref, *strip_refs), (held, acc, full, sems) = (
        refs[: -nband - 6], refs[-nband - 6 : -4], refs[-4:]
    )
    slots = first_ref.shape[0]
    strip_rows = PS // nband
    chunk = slots // 4
    pieces = [(first_ref.at[pl.ds(i, chunk)], i, chunk) for i in range(0, slots, chunk)]
    at = slots
    for ref in second_refs:
        pieces.append((ref, at, ref.shape[0]))
        at += ref.shape[0]
    copies = [
        pltpu.make_async_copy(src, held.at[pl.ds(start, size)], sems.at[i])
        for i, (src, start, size) in enumerate(pieces)
    ]
    for copy in copies:
        copy.start()
    acc[...] = jnp.zeros_like(acc)
    lane = lax.broadcasted_iota(jnp.int32, (8, LANES), 1)
    sub = lax.broadcasted_iota(jnp.int32, (8, LANES), 0)

    def add_tile(index, slot, source):
        code = table_ref[slot, source]

        @pl.when(code > 0)
        def _():
            corner = code - 1
            top = corner // PS
            left = corner & (PS - 1)
            base = pl.multiple_of((top // 8) * 8, 8)
            shift = top & 7
            part = left // LANES
            on = lane >= (left & (LANES - 1))
            tile = held[index].astype(F32)
            for g in range(S // 8):
                rows = tile[8 * g : 8 * g + 8]
                if g == 0:
                    low = jnp.where(sub < shift, rows, 0.0)
                    rows = rows - low
                    at = pl.ds(base + S, 8)
                    acc[part, at, :] += jnp.where(on, low, 0.0)
                    acc[part + 1, at, :] += jnp.where(on, 0.0, low)
                at = pl.ds(base + 8 * g, 8)
                acc[part, at, :] += jnp.where(on, rows, 0.0)
                acc[part + 1, at, :] += jnp.where(on, 0.0, rows)

    for copy, (_, start, size) in zip(copies, pieces):
        copy.wait()

        @pl.loop(0, size, unroll=min(size, 8))
        def _(i):
            if start < slots:
                add_tile(start + i, 0, start + i)
            else:
                source = start - slots + i
                if gathered:
                    source = gathered_source(source, owner_ref[0], slots // PLANE)
                add_tile(start + i, 1, source)

    edge = full.shape[0] - PS
    full[0 : edge // 2, :] = jnp.zeros((edge // 2, PS), F32)
    full[PS + edge // 2 :, :] = jnp.zeros((edge // 2, PS), F32)
    for part in range(PS // LANES):
        at = slice(part * LANES, part * LANES + LANES)
        value = (acc[part, 0:PS, :] * cover_ref[:, at]).astype(BF16)
        coadd_ref[:, at] = value
        full[edge // 2 : edge // 2 + PS, at] = value.astype(F32)
    height = strip_refs[0].shape[0]
    for i, ref in enumerate(strip_refs):
        start = pl.multiple_of((owner_ref[1] ^ i) * strip_rows, 8)
        rows = full[pl.ds(start, height + 8), :]
        ref[...] = rows[edge // 2 - PAD : edge // 2 - PAD + height].astype(BF16)


def place(owner, table, first, seconds, cover, nband, gathered):
    strip = PS // nband + 8
    anywhere = pl.BlockSpec(memory_space=pl.ANY)
    whole = pl.BlockSpec(memory_space=pltpu.VMEM)
    scalars = pl.BlockSpec(memory_space=pltpu.SMEM)
    tiles = first.shape[0] + sum(x.shape[0] for x in seconds)
    return pl.pallas_call(
        lambda *refs: place_kernel(nband, gathered, *refs),
        name="place",
        out_shape=(
            jax.ShapeDtypeStruct((PS, PS), BF16),
            *[jax.ShapeDtypeStruct((strip, PS), BF16)] * nband,
        ),
        in_specs=[scalars, scalars, anywhere, *[anywhere] * len(seconds), whole],
        out_specs=(whole,) * (nband + 1),
        scratch_shapes=[
            pltpu.VMEM((tiles, S, S), BF16),
            pltpu.VMEM((PS // LANES + 1, PS + 8, LANES), F32),
            pltpu.VMEM((PS + 16, PS), F32),
            pltpu.SemaphoreType.DMA((4 + len(seconds),)),
        ],
        compiler_params=pltpu.CompilerParams(vmem_limit_bytes=24 << 20),
    )(owner, table, first, *seconds, cover)


def detect_kernel(nband, *refs):
    strip_refs, (weight_ref, bias_ref, out_ref, main, edge, stage, sems) = (
        refs[:nband], refs[nband:]
    )
    groups = main.shape[0]
    slots, channels, rows, _ = stage.shape
    column = lax.broadcasted_iota(jnp.int32, (8, PS), 1)

    def prepare(g):
        pieces = []
        for s in range(KS):
            for b in range(nband):
                x = strip_refs[b][8 * g : 8 * g + 8, :].astype(F32)
                d = s - PAD
                if d:
                    x = pltpu.roll(x, (-d) % PS, 1)
                    x = jnp.where((column + d >= 0) & (column + d < PS), x, 0.0)
                pieces.append(x)
        if g < groups - 1:
            main[g] = jnp.concatenate(pieces, axis=0).astype(BF16)
        if g:
            edge[g] = jnp.concatenate([x[0:4] for x in pieces], axis=0).astype(BF16)

    def copy(chunk):
        slot = chunk % slots
        return pltpu.make_async_copy(
            stage.at[slot], out_ref.at[:, pl.ds(chunk * rows, rows), :], sems.at[slot]
        )

    prepare(0)
    per_chunk = rows // 8
    chunks = (groups - 1) // per_chunk
    for chunk in range(chunks):
        for i in range(per_chunk):
            prepare(chunk * per_chunk + i + 1)
        if chunk >= slots:
            copy(chunk - slots).wait()
        for i in range(per_chunk):
            g = chunk * per_chunk + i
            rhs = jnp.concatenate([main[g], edge[g + 1]], axis=0)
            res = dot_nn(weight_ref[...], rhs) + bias_ref[...]
            stage[chunk % slots, :, 8 * i : 8 * i + 8, :] = res.reshape(channels, 8, PS).astype(BF16)
        copy(chunk).start()
    for chunk in range(max(0, chunks - slots), chunks):
        copy(chunk).wait()


def detect(strips, weight, bias, channels, strip_rows):
    nband = len(strips)
    groups = strips[0].shape[0] // 8
    depth = nband * KS
    rows, slots = 16, 8
    whole = pl.BlockSpec(memory_space=pltpu.VMEM)
    return pl.pallas_call(
        lambda *refs: detect_kernel(nband, *refs),
        name="detect",
        out_shape=jax.ShapeDtypeStruct((channels, strip_rows, PS), BF16),
        in_specs=[whole] * (nband + 2),
        out_specs=pl.BlockSpec(memory_space=pl.ANY),
        scratch_shapes=[
            pltpu.VMEM((groups, depth * 8, PS), BF16),
            pltpu.VMEM((groups, depth * 4, PS), BF16),
            pltpu.VMEM((slots, channels, rows, PS), BF16),
            pltpu.SemaphoreType.DMA((slots,)),
        ],
        compiler_params=pltpu.CompilerParams(vmem_limit_bytes=24 << 20),
    )(*strips, weight, bias)


def toeplitz(det_weight, nband, band):
    channels, inputs = det_weight.shape
    combos = KS * nband
    column = jnp.arange(combos * 12, dtype=jnp.int32)
    tail = column >= combos * 8
    combo = jnp.where(tail, (column - combos * 8) >> 2, column >> 3)
    row_in = jnp.where(tail, 8 + ((column - combos * 8) & 3), column & 7)
    shift, slot = combo // nband, combo % nband
    source = (slot ^ band) * (KS * KS) + shift
    rows = jnp.arange(KS, dtype=jnp.int32)[:, None] * KS + source[None, :]
    pick = (jnp.arange(inputs, dtype=jnp.int32)[:, None, None] == rows[None]).astype(BF16)
    taps = lax.dot_general(
        det_weight, pick, (((1,), (0,)), ((), ())), preferred_element_type=F32
    )
    offset = row_in[None, :] - jnp.arange(8, dtype=jnp.int32)[:, None]
    total = jnp.zeros((channels, 8, combos * 12), F32)
    for r in range(KS):
        total = jnp.where((offset == r)[None], taps[:, None, r], total)
    return total.astype(BF16).reshape(channels * 8, combos * 12)


def slot_select(targets, capacity):
    counts = jnp.cumsum(targets.astype(jnp.int32), axis=1) - 1
    slot_ids = jnp.arange(capacity, dtype=jnp.int32)
    return targets[None] & (counts[None] == slot_ids[:, None, None])


def body(exposures, psf_taps, warp_rows, warp_cols, routes, offsets, weights, det_weight, det_bias):
    npatch = lax.axis_size("patch")
    nband = lax.axis_size("band")
    tiles = exposures.shape[0]
    capacity = 2
    owner = lax.axis_index("patch").astype(jnp.int32)
    routes_row = routes.transpose(0, 2, 1).reshape(1, -1)
    offs_rows = offsets.transpose(0, 2, 1).reshape(2, -1)
    taps = psf_taps[:, 0].transpose(2, 1, 0).astype(F32)
    inputs = (owner[None], routes_row, offs_rows, weights, taps, exposures, warp_rows, warp_cols)
    extra = repeat(*inputs, npatch, npatch // PLANE)
    lines = [list(range(i, npatch, PLANE)) for i in range(PLANE)]
    near = lax.all_to_all(
        extra, "patch", split_axis=0, concat_axis=0, axis_index_groups=lines, tiled=True
    )
    buf0, buf1 = front(*inputs, npatch)
    buf0, near, routes_row, offs_rows, weights, det_weight, det_bias = lax.optimization_barrier(
        (buf0, near, routes_row, offs_rows, weights, det_weight, det_bias)
    )
    near = [near] + [swap(near, "patch", m) for m in (2, 4, 6)]
    far = [swap(x, "patch", 1) for x in near]
    first = lax.all_to_all(buf0, "patch", split_axis=0, concat_axis=0, tiled=True)
    dest_all = routes_row.reshape(npatch, tiles)
    same = (dest_all[:, :, None] == dest_all[:, None, :]) & (
        jnp.arange(tiles)[None, :, None] > jnp.arange(tiles)[None, None, :]
    )
    repeats = jnp.max(jnp.sum(jnp.any(same, axis=2).astype(F32), axis=1))
    for bit in range(nband.bit_length() - 1):
        repeats = jnp.maximum(repeats, swap(repeats, "band", 1 << bit))
    landed = slot_select(dest_all == owner, capacity)
    corner = (offs_rows[0] * PS + offs_rows[1] + 1).reshape(npatch, tiles)
    table = jnp.sum(jnp.where(landed, corner[None], 0), axis=-1)
    slot_weights = jnp.sum(
        jnp.where(landed, weights.reshape(npatch, tiles)[None], 0.0), axis=-1
    ).reshape(-1)
    slot_corner = jnp.maximum(table.reshape(-1) - 1, 0)
    pixels = jnp.arange(PS, dtype=jnp.int32)
    down = pixels[None, :] - (slot_corner >> (PS.bit_length() - 1))[:, None]
    right = pixels[None, :] - (slot_corner & (PS - 1))[:, None]
    row_cover = jnp.where((down >= 0) & (down < S), slot_weights[:, None], 0.0)
    col_cover = ((right >= 0) & (right < S)).astype(F32)
    cover = jnp.einsum("ky,kx->yx", row_cover, col_cover, precision=lax.Precision.HIGHEST)
    cover = 1.0 / jnp.maximum(cover, 1.0)
    channels = det_weight.shape[0]
    strip_rows = PS // nband
    bias = jnp.broadcast_to(det_bias[:, None, None], (channels, 8, 1)).reshape(channels * 8, 1)
    band = lax.axis_index("band").astype(jnp.int32)
    first, near, far, table, cover, kernel, bias, repeats = lax.optimization_barrier(
        (first, near, far, table, cover, toeplitz(det_weight, nband, band), bias, repeats)
    )
    where = jnp.stack([owner, band])

    def one_repeat():
        return place(where, table, first, (*near, *far), cover, nband, True)

    def any_repeats():
        rest = lax.all_to_all(buf1, "patch", split_axis=0, concat_axis=0, tiled=True)
        return place(where, table, first, (rest,), cover, nband, False)

    coadd, *strips = lax.cond(repeats <= 1.0, one_repeat, any_repeats)
    strips = strips[:1] + [swap(x, "band", i) for i, x in enumerate(strips) if i]
    detection = detect(strips, kernel, bias, channels, strip_rows)
    return (coadd[None, None], detection[None])


def solution(mesh):
    placed = (
        P("patch", "band", None, None),
        P("patch", "band", None, None),
        P("patch", "band", None, None),
        P("patch", "band", None, None),
        P("band", None, None),
        P("band", None, None),
        P("band", None),
        P(),
        P(),
    )
    return jax.shard_map(
        body,
        mesh=mesh,
        in_specs=placed,
        out_specs=(P("patch", "band", None, None), P("patch", None, "band", None)),
        check_vma=False,
    )
```

```python
import jax
import jax.numpy as jnp
from jax import lax
from jax.experimental import pallas as pl
from jax.experimental.pallas import tpu as pltpu
from jax.sharding import PartitionSpec as P

PS = 512
S = 128
TAPS = 7
PLANE = 8
HALF = TAPS // 2
KS = 5
PAD = KS // 2
LANES = 128
F32 = jnp.float32
BF16 = jnp.bfloat16


def dot_nt(a, b):
    return lax.dot_general(a, b, (((1,), (1,)), ((), ())), preferred_element_type=F32)


def dot_nn(a, b):
    return lax.dot_general(a, b, (((1,), (0,)), ((), ())), preferred_element_type=F32)


def warp_tiles(here, base, offs_ref, wts_ref, taps_ref, tiles, rows, cols):
    diag = lax.broadcasted_iota(jnp.int32, (S, S), 1) - lax.broadcasted_iota(jnp.int32, (S, S), 0)

    def band(axis, tile):
        matrix = jnp.zeros((S, S), F32)
        for tap in range(TAPS):
            matrix = jnp.where(diag == tap - HALF, taps_ref[tap, axis, tile], matrix)
        return matrix.astype(BF16)

    each = range(len(here))
    psf_rows = [band(0, t) for t in here]
    psf_cols = [band(1, t) for t in here]
    half_done = [dot_nt(tiles[k], psf_cols[k]).astype(BF16) for k in each]
    matched = [dot_nn(psf_rows[k], half_done[k]).astype(BF16) for k in each]
    across = [dot_nt(matched[k], cols[k]).astype(BF16) for k in each]
    product = [dot_nn(rows[k], across[k]) for k in each]
    out = []
    for k in each:
        place = base + here[k]
        warped = wts_ref[0, place] * product[k]
        warped = pltpu.roll(warped, offs_ref[1, place] & (LANES - 1), 1)
        warped = pltpu.roll(warped, offs_ref[0, place] & 7, 0)
        out.append(warped.astype(BF16))
    return out


def front_kernel(
    part, parts, owner_ref, routes_ref, offs_ref, wts_ref, taps_ref,
    exp_ref, rows_ref, cols_ref, *refs,
):
    *outs, held, stage, count, ranks, found, load_sems, sems = refs[2 * part :]
    buf0_ref, buf1_ref = outs[:2]
    tiles = ranks.shape[0]
    size = stage.shape[0]
    base = owner_ref[0] * tiles
    found[0] = 0

    @pl.loop(0, count.shape[0], unroll=8)
    def _(i):
        count[i] = 0

    @pl.loop(0, tiles, unroll=4)
    def _(i):
        dest = routes_ref[0, base + i]
        rank = count[dest]
        count[dest] = rank + 1
        ranks[i] = rank
        found[0] = jnp.where(rank > 0, i, found[0])

    chosen = found[0]
    here = []
    for n in range(part * size, part * size + size):
        here.append(jnp.where(chosen >= n, n - 1, n) if n else chosen)
    loads = [
        [
            pltpu.make_async_copy(src.at[tile, 0], held.at[i, n], load_sems.at[i, n])
            for i, src in enumerate((exp_ref, rows_ref, cols_ref))
        ]
        for n, tile in enumerate(here)
    ]
    for copies in loads:
        for copy in copies:
            copy.start()
    for copies in loads:
        for copy in copies:
            copy.wait()
    inputs = [[held[i, n] for n in range(size)] for i in range(3)]
    warped = warp_tiles(here, base, offs_ref, wts_ref, taps_ref, *inputs)
    if part == 0:
        outs[2][...] = jnp.broadcast_to(warped[0][None], outs[2].shape)
    for n, value in enumerate(warped):
        stage[n] = value
    for n, tile in enumerate(here):
        dest = routes_ref[0, base + tile]
        rank = ranks[tile]

        @pl.when(rank == 0)
        def _():
            pltpu.make_async_copy(stage.at[n], buf0_ref.at[dest], sems.at[n]).start()

        @pl.when(rank > 0)
        def _():
            pltpu.make_async_copy(stage.at[n], buf1_ref.at[dest], sems.at[n]).start()

    for n in range(size):
        pltpu.make_async_copy(stage.at[n], buf0_ref.at[0], sems.at[n]).wait()


def front(part, inputs, buffers, npatch, copies):
    parts = 2
    tiles = inputs[5].shape[0]
    size = tiles // parts
    anywhere = pl.BlockSpec(memory_space=pl.ANY)
    outside = pl.BlockSpec(memory_space=pltpu.HBM)
    whole = pl.BlockSpec(memory_space=pltpu.VMEM)
    scalars = pl.BlockSpec(memory_space=pltpu.SMEM)
    slots = jax.ShapeDtypeStruct((npatch, S, S), BF16)
    extra = jax.ShapeDtypeStruct((copies, S, S), BF16)
    return pl.pallas_call(
        lambda *refs: front_kernel(part, parts, *refs),
        name="front" + "ab"[part],
        out_shape=(slots, slots) if part else (slots, slots, extra),
        cost_estimate=pl.CostEstimate(flops=0, bytes_accessed=16 << 20, transcendentals=0),
        in_specs=[scalars] * 5 + [anywhere] * 3 + [outside] * len(buffers),
        out_specs=(outside, outside) if part else (outside, outside, whole),
        input_output_aliases={8: 0, 9: 1} if part else {},
        scratch_shapes=[
            pltpu.VMEM((3, size, S, S), BF16),
            pltpu.VMEM((size, S, S), BF16),
            pltpu.SMEM((npatch,), jnp.int32),
            pltpu.SMEM((tiles,), jnp.int32),
            pltpu.SMEM((1,), jnp.int32),
            pltpu.SemaphoreType.DMA((3, size)),
            pltpu.SemaphoreType.DMA((size,)),
        ],
        compiler_params=pltpu.CompilerParams(vmem_limit_bytes=63 << 20),
    )(*inputs, *buffers)


def gathered_source(index, owner, rows):
    step = index // rows
    return (index % rows) * PLANE + (
        (owner % PLANE) ^ (((step & 1) << 1) | ((step & 2) << 1) | ((step & 4) >> 2))
    )


def swap(x, axis, mask):
    size = lax.axis_size(axis)
    return lax.ppermute(x, axis, [(i, i ^ mask) for i in range(size)])


def place_kernel(nband, gathered, owner_ref, table_ref, first_ref, *refs):
    second_refs, (cover_ref, coadd_ref, *strip_refs), (held, acc, full, sems) = (
        refs[: -nband - 6], refs[-nband - 6 : -4], refs[-4:]
    )
    slots = first_ref.shape[0]
    strip_rows = PS // nband
    chunk = slots // 4
    pieces = [(first_ref.at[pl.ds(i, chunk)], i, chunk) for i in range(0, slots, chunk)]
    at = slots
    for ref in second_refs:
        pieces.append((ref, at, ref.shape[0]))
        at += ref.shape[0]
    copies = [
        pltpu.make_async_copy(src, held.at[pl.ds(start, size)], sems.at[i])
        for i, (src, start, size) in enumerate(pieces)
    ]
    for copy in copies:
        copy.start()
    acc[...] = jnp.zeros_like(acc)
    lane = lax.broadcasted_iota(jnp.int32, (8, LANES), 1)
    sub = lax.broadcasted_iota(jnp.int32, (8, LANES), 0)

    def add_tile(index, slot, source):
        code = table_ref[slot, source]

        @pl.when(code > 0)
        def _():
            corner = code - 1
            top = corner // PS
            left = corner & (PS - 1)
            base = pl.multiple_of((top // 8) * 8, 8)
            shift = top & 7
            part = left // LANES
            on = lane >= (left & (LANES - 1))
            tile = held[index].astype(F32)
            for g in range(S // 8):
                rows = tile[8 * g : 8 * g + 8]
                if g == 0:
                    low = jnp.where(sub < shift, rows, 0.0)
                    rows = rows - low
                    at = pl.ds(base + S, 8)
                    acc[part, at, :] += jnp.where(on, low, 0.0)
                    acc[part + 1, at, :] += jnp.where(on, 0.0, low)
                at = pl.ds(base + 8 * g, 8)
                acc[part, at, :] += jnp.where(on, rows, 0.0)
                acc[part + 1, at, :] += jnp.where(on, 0.0, rows)

    for copy, (_, start, size) in zip(copies, pieces):
        copy.wait()

        @pl.loop(0, size, unroll=min(size, 8))
        def _(i):
            if start < slots:
                add_tile(start + i, 0, start + i)
            else:
                source = start - slots + i
                if gathered:
                    source = gathered_source(source, owner_ref[0], slots // PLANE)
                add_tile(start + i, 1, source)

    edge = full.shape[0] - PS
    full[0 : edge // 2, :] = jnp.zeros((edge // 2, PS), F32)
    full[PS + edge // 2 :, :] = jnp.zeros((edge // 2, PS), F32)
    for part in range(PS // LANES):
        at = slice(part * LANES, part * LANES + LANES)
        value = (acc[part, 0:PS, :] * cover_ref[:, at]).astype(BF16)
        coadd_ref[:, at] = value
        full[edge // 2 : edge // 2 + PS, at] = value.astype(F32)
    height = strip_refs[0].shape[0]
    for i, ref in enumerate(strip_refs):
        start = pl.multiple_of((owner_ref[1] ^ i) * strip_rows, 8)
        rows = full[pl.ds(start, height + 8), :]
        ref[...] = rows[edge // 2 - PAD : edge // 2 - PAD + height].astype(BF16)


def place(owner, table, first, seconds, cover, nband, gathered):
    strip = PS // nband + 8
    anywhere = pl.BlockSpec(memory_space=pl.ANY)
    whole = pl.BlockSpec(memory_space=pltpu.VMEM)
    scalars = pl.BlockSpec(memory_space=pltpu.SMEM)
    tiles = first.shape[0] + sum(x.shape[0] for x in seconds)
    return pl.pallas_call(
        lambda *refs: place_kernel(nband, gathered, *refs),
        name="place",
        out_shape=(
            jax.ShapeDtypeStruct((PS, PS), BF16),
            *[jax.ShapeDtypeStruct((strip, PS), BF16)] * nband,
        ),
        in_specs=[scalars, scalars, anywhere, *[anywhere] * len(seconds), whole],
        out_specs=(whole,) * (nband + 1),
        scratch_shapes=[
            pltpu.VMEM((tiles, S, S), BF16),
            pltpu.VMEM((PS // LANES + 1, PS + 8, LANES), F32),
            pltpu.VMEM((PS + 16, PS), F32),
            pltpu.SemaphoreType.DMA((4 + len(seconds),)),
        ],
        compiler_params=pltpu.CompilerParams(vmem_limit_bytes=24 << 20),
    )(owner, table, first, *seconds, cover)


def detect_kernel(nband, *refs):
    strip_refs, (weight_ref, bias_ref, out_ref, main, edge, stage, sems) = (
        refs[:nband], refs[nband:]
    )
    groups = main.shape[0]
    slots, channels, rows, _ = stage.shape
    column = lax.broadcasted_iota(jnp.int32, (8, PS), 1)

    def prepare(g):
        pieces = []
        for s in range(KS):
            for b in range(nband):
                x = strip_refs[b][8 * g : 8 * g + 8, :].astype(F32)
                d = s - PAD
                if d:
                    x = pltpu.roll(x, (-d) % PS, 1)
                    x = jnp.where((column + d >= 0) & (column + d < PS), x, 0.0)
                pieces.append(x)
        if g < groups - 1:
            main[g] = jnp.concatenate(pieces, axis=0).astype(BF16)
        if g:
            edge[g] = jnp.concatenate([x[0:4] for x in pieces], axis=0).astype(BF16)

    def copy(chunk):
        slot = chunk % slots
        return pltpu.make_async_copy(
            stage.at[slot], out_ref.at[:, pl.ds(chunk * rows, rows), :], sems.at[slot]
        )

    prepare(0)
    per_chunk = rows // 8
    chunks = (groups - 1) // per_chunk
    for chunk in range(chunks):
        for i in range(per_chunk):
            prepare(chunk * per_chunk + i + 1)
        if chunk >= slots:
            copy(chunk - slots).wait()
        for i in range(per_chunk):
            g = chunk * per_chunk + i
            rhs = jnp.concatenate([main[g], edge[g + 1]], axis=0)
            res = dot_nn(weight_ref[...], rhs) + bias_ref[...]
            stage[chunk % slots, :, 8 * i : 8 * i + 8, :] = res.reshape(channels, 8, PS).astype(BF16)
        copy(chunk).start()
    for chunk in range(max(0, chunks - slots), chunks):
        copy(chunk).wait()


def detect(strips, weight, bias, channels, strip_rows):
    nband = len(strips)
    groups = strips[0].shape[0] // 8
    depth = nband * KS
    rows, slots = 16, 8
    whole = pl.BlockSpec(memory_space=pltpu.VMEM)
    return pl.pallas_call(
        lambda *refs: detect_kernel(nband, *refs),
        name="detect",
        out_shape=jax.ShapeDtypeStruct((channels, strip_rows, PS), BF16),
        in_specs=[whole] * (nband + 2),
        out_specs=pl.BlockSpec(memory_space=pl.ANY),
        scratch_shapes=[
            pltpu.VMEM((groups, depth * 8, PS), BF16),
            pltpu.VMEM((groups, depth * 4, PS), BF16),
            pltpu.VMEM((slots, channels, rows, PS), BF16),
            pltpu.SemaphoreType.DMA((slots,)),
        ],
        compiler_params=pltpu.CompilerParams(vmem_limit_bytes=24 << 20),
    )(*strips, weight, bias)


def toeplitz(det_weight, nband, band):
    channels, inputs = det_weight.shape
    combos = KS * nband
    column = jnp.arange(combos * 12, dtype=jnp.int32)
    tail = column >= combos * 8
    combo = jnp.where(tail, (column - combos * 8) >> 2, column >> 3)
    row_in = jnp.where(tail, 8 + ((column - combos * 8) & 3), column & 7)
    shift, slot = combo // nband, combo % nband
    source = (slot ^ band) * (KS * KS) + shift
    rows = jnp.arange(KS, dtype=jnp.int32)[:, None] * KS + source[None, :]
    pick = (jnp.arange(inputs, dtype=jnp.int32)[:, None, None] == rows[None]).astype(BF16)
    taps = lax.dot_general(
        det_weight, pick, (((1,), (0,)), ((), ())), preferred_element_type=F32
    )
    offset = row_in[None, :] - jnp.arange(8, dtype=jnp.int32)[:, None]
    total = jnp.zeros((channels, 8, combos * 12), F32)
    for r in range(KS):
        total = jnp.where((offset == r)[None], taps[:, None, r], total)
    return total.astype(BF16).reshape(channels * 8, combos * 12)


def slot_select(targets, capacity):
    counts = jnp.cumsum(targets.astype(jnp.int32), axis=1) - 1
    slot_ids = jnp.arange(capacity, dtype=jnp.int32)
    return targets[None] & (counts[None] == slot_ids[:, None, None])


def body(exposures, psf_taps, warp_rows, warp_cols, routes, offsets, weights, det_weight, det_bias):
    npatch = lax.axis_size("patch")
    nband = lax.axis_size("band")
    tiles = exposures.shape[0]
    capacity = 2
    owner = lax.axis_index("patch").astype(jnp.int32)
    routes_row = routes.transpose(0, 2, 1).reshape(1, -1)
    offs_rows = offsets.transpose(0, 2, 1).reshape(2, -1)
    taps = psf_taps[:, 0].transpose(2, 1, 0).astype(F32)
    inputs = (owner[None], routes_row, offs_rows, weights, taps, exposures, warp_rows, warp_cols)
    buf0, buf1, extra = front(0, inputs, (), npatch, npatch // PLANE)
    lines = [list(range(i, npatch, PLANE)) for i in range(PLANE)]
    near = lax.all_to_all(
        extra, "patch", split_axis=0, concat_axis=0, axis_index_groups=lines, tiled=True
    )
    buf0, buf1 = front(1, inputs, (buf0, buf1), npatch, npatch // PLANE)
    buf0, near, routes_row, offs_rows, weights, det_weight, det_bias = lax.optimization_barrier(
        (buf0, near, routes_row, offs_rows, weights, det_weight, det_bias)
    )
    near = [near] + [swap(near, "patch", m) for m in (2, 4, 6)]
    far = [swap(x, "patch", 1) for x in near]
    first = lax.all_to_all(buf0, "patch", split_axis=0, concat_axis=0, tiled=True)
    dest_all = routes_row.reshape(npatch, tiles)
    same = (dest_all[:, :, None] == dest_all[:, None, :]) & (
        jnp.arange(tiles)[None, :, None] > jnp.arange(tiles)[None, None, :]
    )
    repeats = jnp.max(jnp.sum(jnp.any(same, axis=2).astype(F32), axis=1))
    for bit in range(nband.bit_length() - 1):
        repeats = jnp.maximum(repeats, swap(repeats, "band", 1 << bit))
    landed = slot_select(dest_all == owner, capacity)
    corner = (offs_rows[0] * PS + offs_rows[1] + 1).reshape(npatch, tiles)
    table = jnp.sum(jnp.where(landed, corner[None], 0), axis=-1)
    slot_weights = jnp.sum(
        jnp.where(landed, weights.reshape(npatch, tiles)[None], 0.0), axis=-1
    ).reshape(-1)
    slot_corner = jnp.maximum(table.reshape(-1) - 1, 0)
    pixels = jnp.arange(PS, dtype=jnp.int32)
    down = pixels[None, :] - (slot_corner >> (PS.bit_length() - 1))[:, None]
    right = pixels[None, :] - (slot_corner & (PS - 1))[:, None]
    row_cover = jnp.where((down >= 0) & (down < S), slot_weights[:, None], 0.0)
    col_cover = ((right >= 0) & (right < S)).astype(F32)
    cover = jnp.einsum("ky,kx->yx", row_cover, col_cover, precision=lax.Precision.HIGHEST)
    cover = 1.0 / jnp.maximum(cover, 1.0)
    channels = det_weight.shape[0]
    strip_rows = PS // nband
    bias = jnp.broadcast_to(det_bias[:, None, None], (channels, 8, 1)).reshape(channels * 8, 1)
    band = lax.axis_index("band").astype(jnp.int32)
    first, near, far, table, cover, kernel, bias, repeats = lax.optimization_barrier(
        (first, near, far, table, cover, toeplitz(det_weight, nband, band), bias, repeats)
    )
    where = jnp.stack([owner, band])

    def one_repeat():
        return place(where, table, first, (*near, *far), cover, nband, True)

    def any_repeats():
        rest = lax.all_to_all(buf1, "patch", split_axis=0, concat_axis=0, tiled=True)
        return place(where, table, first, (rest,), cover, nband, False)

    coadd, *strips = lax.cond(repeats <= 1.0, one_repeat, any_repeats)
    strips = strips[:1] + [swap(x, "band", i) for i, x in enumerate(strips) if i]
    detection = detect(strips, kernel, bias, channels, strip_rows)
    return (coadd[None, None], detection[None])


def solution(mesh):
    placed = (
        P("patch", "band", None, None),
        P("patch", "band", None, None),
        P("patch", "band", None, None),
        P("patch", "band", None, None),
        P("band", None, None),
        P("band", None, None),
        P("band", None),
        P(),
        P(),
    )
    return jax.shard_map(
        body,
        mesh=mesh,
        in_specs=placed,
        out_specs=(P("patch", "band", None, None), P("patch", None, "band", None)),
        check_vma=False,
    )
```

```python
import jax
import jax.numpy as jnp
from jax import lax
from jax.experimental import pallas as pl
from jax.experimental.pallas import tpu as pltpu
from jax.sharding import PartitionSpec as P

PS = 512
S = 128
TAPS = 7
PLANE = 8
HALF = TAPS // 2
KS = 5
PAD = KS // 2
LANES = 128
F32 = jnp.float32
BF16 = jnp.bfloat16


def dot_nt(a, b):
    return lax.dot_general(a, b, (((1,), (1,)), ((), ())), preferred_element_type=F32)


def dot_nn(a, b):
    return lax.dot_general(a, b, (((1,), (0,)), ((), ())), preferred_element_type=F32)


def warp_tiles(here, base, offs_ref, wts_ref, taps_ref, tiles, rows, cols):
    diag = lax.broadcasted_iota(jnp.int32, (S, S), 1) - lax.broadcasted_iota(jnp.int32, (S, S), 0)

    def band(axis, tile):
        matrix = jnp.zeros((S, S), F32)
        for tap in range(TAPS):
            matrix = jnp.where(diag == tap - HALF, taps_ref[tap, axis, tile], matrix)
        return matrix.astype(BF16)

    each = range(len(here))
    psf_rows = [band(0, t) for t in here]
    psf_cols = [band(1, t) for t in here]
    half_done = [dot_nt(tiles[k], psf_cols[k]).astype(BF16) for k in each]
    matched = [dot_nn(psf_rows[k], half_done[k]).astype(BF16) for k in each]
    across = [dot_nt(matched[k], cols[k]).astype(BF16) for k in each]
    product = [dot_nn(rows[k], across[k]) for k in each]
    out = []
    for k in each:
        place = base + here[k]
        warped = wts_ref[0, place] * product[k]
        warped = pltpu.roll(warped, offs_ref[1, place] & (LANES - 1), 1)
        warped = pltpu.roll(warped, offs_ref[0, place] & 7, 0)
        out.append(warped.astype(BF16))
    return out


def own_entries(owner_ref, sources, targets, sems, tiles):
    per_row = LANES // tiles
    start = pl.multiple_of((owner_ref[0] // per_row) * LANES, LANES)
    copies = [
        pltpu.make_async_copy(src.at[:, pl.ds(start, LANES)], dst, sems.at[i])
        for i, (src, dst) in enumerate(zip(sources, targets))
    ]
    for copy in copies:
        copy.start()
    for copy in copies:
        copy.wait()
    return (owner_ref[0] % per_row) * tiles


def own_scratch():
    return [
        pltpu.SMEM((1, LANES), jnp.int32),
        pltpu.SMEM((2, LANES), jnp.int32),
        pltpu.SMEM((1, LANES), F32),
        pltpu.SemaphoreType.DMA((3,)),
    ]


def repeat_kernel(
    tiles, owner_ref, all_routes, all_offs, all_wts, taps_ref,
    exp_ref, rows_ref, cols_ref, out_ref, held, count, found, sems,
    routes_ref, offs_ref, wts_ref, own_sems,
):
    base = own_entries(
        owner_ref, (all_routes, all_offs, all_wts), (routes_ref, offs_ref, wts_ref), own_sems, tiles
    )
    found[0] = 0

    @pl.loop(0, count.shape[0], unroll=8)
    def _(i):
        count[i] = 0

    @pl.loop(0, tiles, unroll=4)
    def _(i):
        dest = routes_ref[0, base + i]
        rank = count[dest]
        count[dest] = rank + 1
        found[0] = jnp.where(rank > 0, i, found[0])

    tile = found[0]
    copies = [
        pltpu.make_async_copy(src.at[tile, 0], held.at[i], sems.at[i])
        for i, src in enumerate((exp_ref, rows_ref, cols_ref))
    ]
    for copy in copies:
        copy.start()
    for copy in copies:
        copy.wait()
    warped = warp_tiles(
        [tile], base, offs_ref, wts_ref, taps_ref, [held[0]], [held[1]], [held[2]]
    )
    out_ref[...] = jnp.broadcast_to(warped[0][None], out_ref.shape)


def repeat(owner, routes, offs, wts, taps, exposures, warp_rows, warp_cols, npatch, copies):
    anywhere = pl.BlockSpec(memory_space=pl.ANY)
    scalars = pl.BlockSpec(memory_space=pltpu.SMEM)
    return pl.pallas_call(
        lambda *refs: repeat_kernel(exposures.shape[0], *refs),
        name="repeat",
        out_shape=jax.ShapeDtypeStruct((copies, S, S), BF16),
        in_specs=[scalars, anywhere, anywhere, anywhere, scalars] + [anywhere] * 3,
        out_specs=pl.BlockSpec(memory_space=pltpu.VMEM),
        scratch_shapes=[
            pltpu.VMEM((3, S, S), BF16),
            pltpu.SMEM((npatch,), jnp.int32),
            pltpu.SMEM((1,), jnp.int32),
            pltpu.SemaphoreType.DMA((3,)),
            *own_scratch(),
        ],
    )(owner, routes, offs, wts, taps, exposures, warp_rows, warp_cols)


def front_kernel(
    chunk, owner_ref, all_routes, all_offs, all_wts, taps_ref,
    exp_ref, rows_ref, cols_ref, buf0_ref, buf1_ref, held, stage, count, load_sems, sems,
    routes_ref, offs_ref, wts_ref, own_sems,
):
    tiles = stage.shape[0]
    loads = [
        [
            pltpu.make_async_copy(
                src.at[pl.ds(start, chunk), 0], held.at[i, pl.ds(start, chunk)], load_sems.at[i, n]
            )
            for i, src in enumerate((exp_ref, rows_ref, cols_ref))
        ]
        for n, start in enumerate(range(0, tiles, chunk))
    ]
    for copies in loads:
        for copy in copies:
            copy.start()

    @pl.loop(0, count.shape[0], unroll=8)
    def _(i):
        count[i] = 0

    base = own_entries(
        owner_ref, (all_routes, all_offs, all_wts), (routes_ref, offs_ref, wts_ref), own_sems, tiles
    )
    for n, copies in enumerate(loads):
        for copy in copies:
            copy.wait()
        here = [n * chunk + k for k in range(chunk)]
        inputs = [[held[i, tile] for tile in here] for i in range(3)]
        warped = warp_tiles(here, base, offs_ref, wts_ref, taps_ref, *inputs)
        for tile, value in zip(here, warped):
            stage[tile] = value
        for tile in here:
            dest = routes_ref[0, base + tile]
            rank = count[dest]
            count[dest] = rank + 1

            @pl.when(rank == 0)
            def _():
                pltpu.make_async_copy(stage.at[tile], buf0_ref.at[dest], sems.at[tile]).start()

            @pl.when(rank > 0)
            def _():
                pltpu.make_async_copy(stage.at[tile], buf1_ref.at[dest], sems.at[tile]).start()

    @pl.loop(0, tiles, unroll=8)
    def _(i):
        pltpu.make_async_copy(stage.at[i], buf0_ref.at[0], sems.at[i]).wait()


def front(owner, routes, offs, wts, taps, exposures, warp_rows, warp_cols, npatch):
    tiles = exposures.shape[0]
    chunk = 16
    anywhere = pl.BlockSpec(memory_space=pl.ANY)
    scalars = pl.BlockSpec(memory_space=pltpu.SMEM)
    return pl.pallas_call(
        lambda *refs: front_kernel(chunk, *refs),
        name="front",
        out_shape=(
            jax.ShapeDtypeStruct((npatch, S, S), BF16),
            jax.ShapeDtypeStruct((npatch, S, S), BF16),
        ),
        cost_estimate=pl.CostEstimate(flops=0, bytes_accessed=24 << 20, transcendentals=0),
        in_specs=[scalars, anywhere, anywhere, anywhere, scalars] + [anywhere] * 3,
        out_specs=(anywhere, anywhere),
        scratch_shapes=[
            pltpu.VMEM((3, tiles, S, S), BF16),
            pltpu.VMEM((tiles, S, S), BF16),
            pltpu.SMEM((npatch,), jnp.int32),
            pltpu.SemaphoreType.DMA((3, tiles // chunk)),
            pltpu.SemaphoreType.DMA((tiles,)),
            *own_scratch(),
        ],
    )(owner, routes, offs, wts, taps, exposures, warp_rows, warp_cols)


def gathered_source(index, owner, rows):
    step = index // rows
    return (index % rows) * PLANE + (
        (owner % PLANE) ^ (((step & 1) << 1) | ((step & 2) << 1) | ((step & 4) >> 2))
    )


def swap(x, axis, mask):
    size = lax.axis_size(axis)
    return lax.ppermute(x, axis, [(i, i ^ mask) for i in range(size)])


def place_kernel(nband, gathered, owner_ref, table_ref, first_ref, *refs):
    second_refs, (cover_ref, coadd_ref, *strip_refs), (held, acc, full, sems) = (
        refs[: -nband - 6], refs[-nband - 6 : -4], refs[-4:]
    )
    slots = first_ref.shape[0]
    strip_rows = PS // nband
    chunk = slots // 4
    pieces = [(first_ref.at[pl.ds(i, chunk)], i, chunk) for i in range(0, slots, chunk)]
    at = slots
    for ref in second_refs:
        pieces.append((ref, at, ref.shape[0]))
        at += ref.shape[0]
    copies = [
        pltpu.make_async_copy(src, held.at[pl.ds(start, size)], sems.at[i])
        for i, (src, start, size) in enumerate(pieces)
    ]
    for copy in copies:
        copy.start()
    acc[...] = jnp.zeros_like(acc)
    lane = lax.broadcasted_iota(jnp.int32, (8, LANES), 1)
    sub = lax.broadcasted_iota(jnp.int32, (8, LANES), 0)

    def add_tile(index, slot, source):
        code = table_ref[slot, source]

        @pl.when(code > 0)
        def _():
            corner = code - 1
            top = corner // PS
            left = corner & (PS - 1)
            base = pl.multiple_of((top // 8) * 8, 8)
            shift = top & 7
            part = left // LANES
            on = lane >= (left & (LANES - 1))
            tile = held[index].astype(F32)
            for g in range(S // 8):
                rows = tile[8 * g : 8 * g + 8]
                if g == 0:
                    low = jnp.where(sub < shift, rows, 0.0)
                    rows = rows - low
                    at = pl.ds(base + S, 8)
                    acc[part, at, :] += jnp.where(on, low, 0.0)
                    acc[part + 1, at, :] += jnp.where(on, 0.0, low)
                at = pl.ds(base + 8 * g, 8)
                acc[part, at, :] += jnp.where(on, rows, 0.0)
                acc[part + 1, at, :] += jnp.where(on, 0.0, rows)

    for copy, (_, start, size) in zip(copies, pieces):
        copy.wait()

        @pl.loop(0, size, unroll=min(size, 8))
        def _(i):
            if start < slots:
                add_tile(start + i, 0, start + i)
            else:
                source = start - slots + i
                if gathered:
                    source = gathered_source(source, owner_ref[0], slots // PLANE)
                add_tile(start + i, 1, source)

    edge = full.shape[0] - PS
    full[0 : edge // 2, :] = jnp.zeros((edge // 2, PS), F32)
    full[PS + edge // 2 :, :] = jnp.zeros((edge // 2, PS), F32)
    for part in range(PS // LANES):
        at = slice(part * LANES, part * LANES + LANES)
        value = (acc[part, 0:PS, :] * cover_ref[:, at]).astype(BF16)
        coadd_ref[:, at] = value
        full[edge // 2 : edge // 2 + PS, at] = value.astype(F32)
    height = strip_refs[0].shape[0]
    for i, ref in enumerate(strip_refs):
        start = pl.multiple_of((owner_ref[1] ^ i) * strip_rows, 8)
        rows = full[pl.ds(start, height + 8), :]
        ref[...] = rows[edge // 2 - PAD : edge // 2 - PAD + height].astype(BF16)


def place(owner, table, first, seconds, cover, nband, gathered):
    strip = PS // nband + 8
    anywhere = pl.BlockSpec(memory_space=pl.ANY)
    whole = pl.BlockSpec(memory_space=pltpu.VMEM)
    scalars = pl.BlockSpec(memory_space=pltpu.SMEM)
    tiles = first.shape[0] + sum(x.shape[0] for x in seconds)
    return pl.pallas_call(
        lambda *refs: place_kernel(nband, gathered, *refs),
        name="place",
        out_shape=(
            jax.ShapeDtypeStruct((PS, PS), BF16),
            *[jax.ShapeDtypeStruct((strip, PS), BF16)] * nband,
        ),
        in_specs=[scalars, scalars, anywhere, *[anywhere] * len(seconds), whole],
        out_specs=(whole,) * (nband + 1),
        scratch_shapes=[
            pltpu.VMEM((tiles, S, S), BF16),
            pltpu.VMEM((PS // LANES + 1, PS + 8, LANES), F32),
            pltpu.VMEM((PS + 16, PS), F32),
            pltpu.SemaphoreType.DMA((4 + len(seconds),)),
        ],
        compiler_params=pltpu.CompilerParams(vmem_limit_bytes=24 << 20),
    )(owner, table, first, *seconds, cover)


def detect_kernel(nband, *refs):
    strip_refs, (weight_ref, bias_ref, out_ref, main, edge, stage, sems) = (
        refs[:nband], refs[nband:]
    )
    groups = main.shape[0]
    slots, channels, rows, _ = stage.shape
    column = lax.broadcasted_iota(jnp.int32, (8, PS), 1)

    def prepare(g):
        pieces = []
        for s in range(KS):
            for b in range(nband):
                x = strip_refs[b][8 * g : 8 * g + 8, :].astype(F32)
                d = s - PAD
                if d:
                    x = pltpu.roll(x, (-d) % PS, 1)
                    x = jnp.where((column + d >= 0) & (column + d < PS), x, 0.0)
                pieces.append(x)
        if g < groups - 1:
            main[g] = jnp.concatenate(pieces, axis=0).astype(BF16)
        if g:
            edge[g] = jnp.concatenate([x[0:4] for x in pieces], axis=0).astype(BF16)

    def copy(chunk):
        slot = chunk % slots
        return pltpu.make_async_copy(
            stage.at[slot], out_ref.at[:, pl.ds(chunk * rows, rows), :], sems.at[slot]
        )

    prepare(0)
    per_chunk = rows // 8
    chunks = (groups - 1) // per_chunk
    for chunk in range(chunks):
        for i in range(per_chunk):
            prepare(chunk * per_chunk + i + 1)
        if chunk >= slots:
            copy(chunk - slots).wait()
        for i in range(per_chunk):
            g = chunk * per_chunk + i
            rhs = jnp.concatenate([main[g], edge[g + 1]], axis=0)
            res = dot_nn(weight_ref[...], rhs) + bias_ref[...]
            stage[chunk % slots, :, 8 * i : 8 * i + 8, :] = res.reshape(channels, 8, PS).astype(BF16)
        copy(chunk).start()
    for chunk in range(max(0, chunks - slots), chunks):
        copy(chunk).wait()


def detect(strips, weight, bias, channels, strip_rows):
    nband = len(strips)
    groups = strips[0].shape[0] // 8
    depth = nband * KS
    rows, slots = 16, 8
    whole = pl.BlockSpec(memory_space=pltpu.VMEM)
    return pl.pallas_call(
        lambda *refs: detect_kernel(nband, *refs),
        name="detect",
        out_shape=jax.ShapeDtypeStruct((channels, strip_rows, PS), BF16),
        in_specs=[whole] * (nband + 2),
        out_specs=pl.BlockSpec(memory_space=pl.ANY),
        scratch_shapes=[
            pltpu.VMEM((groups, depth * 8, PS), BF16),
            pltpu.VMEM((groups, depth * 4, PS), BF16),
            pltpu.VMEM((slots, channels, rows, PS), BF16),
            pltpu.SemaphoreType.DMA((slots,)),
        ],
        compiler_params=pltpu.CompilerParams(vmem_limit_bytes=24 << 20),
    )(*strips, weight, bias)


def toeplitz(det_weight, nband, band):
    channels, inputs = det_weight.shape
    combos = KS * nband
    column = jnp.arange(combos * 12, dtype=jnp.int32)
    tail = column >= combos * 8
    combo = jnp.where(tail, (column - combos * 8) >> 2, column >> 3)
    row_in = jnp.where(tail, 8 + ((column - combos * 8) & 3), column & 7)
    shift, slot = combo // nband, combo % nband
    source = (slot ^ band) * (KS * KS) + shift
    rows = jnp.arange(KS, dtype=jnp.int32)[:, None] * KS + source[None, :]
    pick = (jnp.arange(inputs, dtype=jnp.int32)[:, None, None] == rows[None]).astype(BF16)
    taps = lax.dot_general(
        det_weight, pick, (((1,), (0,)), ((), ())), preferred_element_type=F32
    )
    offset = row_in[None, :] - jnp.arange(8, dtype=jnp.int32)[:, None]
    total = jnp.zeros((channels, 8, combos * 12), F32)
    for r in range(KS):
        total = jnp.where((offset == r)[None], taps[:, None, r], total)
    return total.astype(BF16).reshape(channels * 8, combos * 12)


def slot_select(targets, capacity):
    counts = jnp.cumsum(targets.astype(jnp.int32), axis=1) - 1
    slot_ids = jnp.arange(capacity, dtype=jnp.int32)
    return targets[None] & (counts[None] == slot_ids[:, None, None])


def body(exposures, psf_taps, warp_rows, warp_cols, routes, offsets, weights, det_weight, det_bias):
    npatch = lax.axis_size("patch")
    nband = lax.axis_size("band")
    tiles = exposures.shape[0]
    capacity = 2
    owner = lax.axis_index("patch").astype(jnp.int32)
    routes_row = routes.transpose(0, 2, 1).reshape(1, -1)
    offs_rows = offsets.transpose(0, 2, 1).reshape(2, -1)
    taps = psf_taps[:, 0].transpose(2, 1, 0).astype(F32)
    inputs = (owner[None], routes_row, offs_rows, weights, taps, exposures, warp_rows, warp_cols)
    extra = repeat(*inputs, npatch, npatch // PLANE)
    lines = [list(range(i, npatch, PLANE)) for i in range(PLANE)]
    near = lax.all_to_all(
        extra, "patch", split_axis=0, concat_axis=0, axis_index_groups=lines, tiled=True
    )
    buf0, buf1 = front(*inputs, npatch)
    buf0, near, routes_row, offs_rows, weights, det_weight, det_bias = lax.optimization_barrier(
        (buf0, near, routes_row, offs_rows, weights, det_weight, det_bias)
    )
    near = [near] + [swap(near, "patch", m) for m in (2, 4, 6)]
    far = [swap(x, "patch", 1) for x in near]
    first = lax.all_to_all(buf0, "patch", split_axis=0, concat_axis=0, tiled=True)
    dest_all = routes_row.reshape(npatch, tiles)
    same = (dest_all[:, :, None] == dest_all[:, None, :]) & (
        jnp.arange(tiles)[None, :, None] > jnp.arange(tiles)[None, None, :]
    )
    repeats = jnp.max(jnp.sum(jnp.any(same, axis=2).astype(F32), axis=1))
    for bit in range(nband.bit_length() - 1):
        repeats = jnp.maximum(repeats, swap(repeats, "band", 1 << bit))
    landed = slot_select(dest_all == owner, capacity)
    corner = (offs_rows[0] * PS + offs_rows[1] + 1).reshape(npatch, tiles)
    table = jnp.sum(jnp.where(landed, corner[None], 0), axis=-1)
    slot_weights = jnp.sum(
        jnp.where(landed, weights.reshape(npatch, tiles)[None], 0.0), axis=-1
    ).reshape(-1)
    slot_corner = jnp.maximum(table.reshape(-1) - 1, 0)
    pixels = jnp.arange(PS, dtype=jnp.int32)
    down = pixels[None, :] - (slot_corner >> (PS.bit_length() - 1))[:, None]
    right = pixels[None, :] - (slot_corner & (PS - 1))[:, None]
    row_cover = jnp.where((down >= 0) & (down < S), slot_weights[:, None], 0.0)
    col_cover = ((right >= 0) & (right < S)).astype(F32)
    cover = jnp.einsum("ky,kx->yx", row_cover, col_cover, precision=lax.Precision.HIGHEST)
    cover = 1.0 / jnp.maximum(cover, 1.0)
    channels = det_weight.shape[0]
    strip_rows = PS // nband
    bias = jnp.broadcast_to(det_bias[:, None, None], (channels, 8, 1)).reshape(channels * 8, 1)
    band = lax.axis_index("band").astype(jnp.int32)
    first, near, far, table, cover, kernel, bias, repeats = lax.optimization_barrier(
        (first, near, far, table, cover, toeplitz(det_weight, nband, band), bias, repeats)
    )
    where = jnp.stack([owner, band])

    def one_repeat():
        return place(where, table, first, (*near, *far), cover, nband, True)

    def any_repeats():
        rest = lax.all_to_all(buf1, "patch", split_axis=0, concat_axis=0, tiled=True)
        return place(where, table, first, (rest,), cover, nband, False)

    coadd, *strips = lax.cond(repeats <= 1.0, one_repeat, any_repeats)
    strips = strips[:1] + [swap(x, "band", i) for i, x in enumerate(strips) if i]
    detection = detect(strips, kernel, bias, channels, strip_rows)
    return (coadd[None, None], detection[None])


def solution(mesh):
    placed = (
        P("patch", "band", None, None),
        P("patch", "band", None, None),
        P("patch", "band", None, None),
        P("patch", "band", None, None),
        P("band", None, None),
        P("band", None, None),
        P("band", None),
        P(),
        P(),
    )
    return jax.shard_map(
        body,
        mesh=mesh,
        in_specs=placed,
        out_specs=(P("patch", "band", None, None), P("patch", None, "band", None)),
        check_vma=False,
    )
```
